512 devices in a mesh: group: 32 (over x, z), shard: 16 (over y, core).
Axes of the slice: x: 4, y: 8, z: 8, core: 2. Of those that a mesh axis runs over, the one named last changes fastest.
Arguments:
- tokens: bfloat16 [1024, 1024], P(('group', 'shard')), may hold values from -6 to 6
- norm_gain: float32 [1024], replicated, may hold values from 0.5 to 1.5
- qkv_weight: bfloat16 [1024, 3072], P(None, 'shard'), may hold values from -0.1875 to 0.1875
- conv_weight: float32 [4, 3072], P(None, 'shard'), may hold values from -3 to 3
- conv_state: bfloat16 [1024, 3, 3072], P('group', None, 'shard'), may hold values from -6 to 6
- mesa_gates: bfloat16 [1024, 16], replicated, may hold values from -0.1875 to 0.1875
- mesa_bias: float32 [16], replicated, may hold values from -3 to 3
- ridge_term: float32 [8], replicated, may hold values from 0.5 to 2
- key_cache: bfloat16 [2048, 128, 1024], P(('group', 'shard')), may hold values from -1.25 to 1.25
- value_cache: bfloat16 [2048, 128, 1024], P(('group', 'shard')), may hold values from -6 to 6
- log_weight: bfloat16 [2048, 8, 128], P(('group', 'shard'))
- page_owner: int32 [2048], P(('group', 'shard')), may hold values from 0 to 63, as said below
- page_fill: int32 [2048], P(('group', 'shard')), may hold values from 1 to 128, as said below
- out_weight: bfloat16 [1024, 1024], P('shard'), may hold values from -0.1875 to 0.1875
- mlp_gain: float32 [1024], replicated, may hold values from 0.5 to 1.5
- gate_weight: bfloat16 [1024, 2816], P(None, 'shard'), may hold values from -0.1875 to 0.1875
- up_weight: bfloat16 [1024, 2816], P(None, 'shard'), may hold values from -0.1875 to 0.1875
- down_weight: bfloat16 [2816, 1024], P('shard'), may hold values from -0.109375 to 0.109375
Outputs:
- retrieved: bfloat16 [1024, 1024], P(('group', 'shard'))
- layer_out: bfloat16 [1024, 1024], P(('group', 'shard'))
The draws below stay inside these ranges and needn't reach their ends.
Inputs may be any that keep to these rules, and one draw needn't show every extreme that they name: `page_owner`: slots of a pair of groups (groups 2p and 2p + 1) belong to that pair's requests: 0 to 31 are group 2p's requests in row order, 32 to 63 group 2p + 1's. Every slot is owned, every request owns one or more slots, and a request's slots may lie on any device of either group of its pair. `page_fill`: tokens stored from the start of the slot; only a request's last page may be partly filled.
All inputs are finite; a program needn't handle non-finite values.
Results may differ from the reference program's by a relative error of at most 0.0085.
Values may be sent and summed in bfloat16 or wider, within the bound.
A program may use at most 64 MiB of HBM per device.

```python
import math
import jax
import jax.numpy as jnp
from jax import lax

D = 1024
ATTENTION_COUNT = 8
DH = 128
FF = 2816
PAGE = 128
CONV = 4
ITERS = 4
COUPLED_QUERIES = 64
REQUESTS = 1024
SLOTS_PAIR = 128
PAGES = 2048
MOST = 32
N_GROUP = 32


def pair_layout(key):
    base_key = jax.random.fold_in(key, 101)
    spare_pages = SLOTS_PAIR - MOST - (COUPLED_QUERIES - 1)

    def one_pair(pair_index):
        pair_key = jax.random.fold_in(base_key, pair_index)
        sub_keys = jax.random.split(pair_key, 5)
        order = jax.random.permutation(sub_keys[0], COUPLED_QUERIES)
        longest = order[COUPLED_QUERIES - 1]
        others = order[:COUPLED_QUERIES - 1]
        upper = jax.random.randint(sub_keys[1], (spare_pages,), 1, COUPLED_QUERIES)
        picks = jax.random.randint(sub_keys[2], (spare_pages,), 0, upper)
        chosen = others[picks]
        members = jnp.arange(COUPLED_QUERIES)
        extra = jnp.sum((chosen[:, None] == members[None, :]).astype(jnp.int32), axis=0)
        counts = jnp.where(members == longest, MOST, 1 + extra).astype(jnp.int32)
        starts = jnp.cumsum(counts) - counts
        places = jnp.arange(SLOTS_PAIR)
        owner_seq = jnp.sum((starts[None, :] <= places[:, None]).astype(jnp.int32), axis=1) - 1
        rank_seq = places - starts[owner_seq]
        last_fill = jax.random.randint(sub_keys[3], (COUPLED_QUERIES,), 1, PAGE + 1)
        fill_seq = jnp.where(rank_seq == counts[owner_seq] - 1, last_fill[owner_seq], PAGE)
        overall_extent = (counts - 1) * PAGE + last_fill
        spots = jax.random.permutation(sub_keys[4], SLOTS_PAIR)
        inverse = jnp.argsort(spots)
        return (owner_seq[inverse].astype(jnp.int32), fill_seq[inverse].astype(jnp.int32), rank_seq[inverse].astype(jnp.int32), overall_extent.astype(jnp.int32))
    return jax.vmap(one_pair)(jnp.arange(N_GROUP // 2))


def draw_page_owner(key, part):
    holder_sequence, fill, rank, overall_extent = pair_layout(key)
    return holder_sequence.reshape(-1).astype(jnp.int32)


def draw_page_fill(key, part):
    holder_sequence, fill, rank, overall_extent = pair_layout(key)
    return fill.reshape(-1).astype(jnp.int32)


def draw_log_weight(key, part):
    holder_sequence, fill, rank, overall_extent = pair_layout(key)
    couple_number = N_GROUP // 2
    lookup_vectors_real = jax.random.split(jax.random.fold_in(key, 202), 4)
    rates = jnp.exp(jax.random.uniform(lookup_vectors_real[0], (couple_number, COUPLED_QUERIES, ATTENTION_COUNT), minval=math.log(0.0003), maxval=math.log(0.03)))
    keep_part = jax.random.uniform(lookup_vectors_real[1], (couple_number, SLOTS_PAIR, ATTENTION_COUNT, PAGE), minval=0.1, maxval=1.0)
    contiguous_spans = jax.random.randint(lookup_vectors_real[2], (couple_number, COUPLED_QUERIES, ATTENTION_COUNT, 3), 0, overall_extent[:, :, None, None])
    depths = jax.random.uniform(lookup_vectors_real[3], (couple_number, COUPLED_QUERIES, ATTENTION_COUNT, 3), minval=0.22, maxval=0.69)
    slot_rate = jnp.take_along_axis(rates, holder_sequence[:, :, None], axis=1)
    slot_total = jnp.take_along_axis(overall_extent, holder_sequence, axis=1)
    entry_contiguous_spans = jnp.take_along_axis(contiguous_spans, holder_sequence[:, :, None, None], axis=1)
    slot_depths = jnp.take_along_axis(depths, holder_sequence[:, :, None, None], axis=1)
    sequence_offset = rank[:, :, None] * PAGE + jnp.arange(PAGE)[None, None, :]
    distance = jnp.maximum(slot_total[:, :, None] - 1 - sequence_offset, 0).astype(jnp.float32)
    log_decay = -slot_rate[:, :, :, None] * distance[:, :, None, :]
    equality_indicator = (sequence_offset[:, :, None, :, None] < entry_contiguous_spans[:, :, :, None, :]).astype(jnp.float32)
    lost = jnp.sum(equality_indicator * slot_depths[:, :, :, None, :], axis=-1)
    values = jnp.log(keep_part) + log_decay - lost
    return values.reshape(couple_number * SLOTS_PAIR, ATTENTION_COUNT, PAGE).astype(jnp.bfloat16)


def block_scale(stream_key, dims, cuts, smallest, high):
    factor_of = 1.0
    for position, parts in cuts:
        steps = jax.random.uniform(jax.random.fold_in(jax.random.fold_in(stream_key, 6), position), (parts,), jnp.float32, smallest / len(cuts), high / len(cuts))
        factor_of = factor_of * jnp.repeat(jnp.exp(steps), dims[position] // parts).reshape((-1,) + (1,) * (len(dims) - 1 - position))
    return factor_of


def scatter_about(stream_key, dims, scale, bound, pieces=(), held_as=jnp.bfloat16):
    level = block_scale(stream_key, dims, pieces, -0.22, 0.18) if pieces else 1.0
    values = jax.random.normal(stream_key, dims, jnp.float32) * scale * level
    return jnp.minimum(jnp.maximum(values, -bound), bound).astype(held_as)


def setup_inputs(seed: int = 0) -> dict:
    splits = jax.random.split(jax.random.key(seed), 19)
    tokens = scatter_about(splits[0], (REQUESTS, D), 1.0, 6.0, ((0, 512),))
    norm_gain = jnp.clip(1.0 + 0.1 * jax.random.normal(splits[1], (D,), jnp.float32), 0.5, 1.5)
    qkv_weight = scatter_about(splits[2], (D, 3 * ATTENTION_COUNT * DH), D ** -0.5, 0.1875, ((1, 16),))
    conv_weight = scatter_about(splits[3], (CONV, 3 * ATTENTION_COUNT * DH), 0.5, 3.0, ((1, 16),), jnp.float32)
    conv_state = scatter_about(splits[4], (REQUESTS, CONV - 1, 3 * ATTENTION_COUNT * DH), 1.0, 6.0, ((0, 32), (2, 16)))
    mesa_gates = scatter_about(splits[5], (D, 2 * ATTENTION_COUNT), D ** -0.5, 0.1875)
    mesa_bias = scatter_about(splits[6], (2 * ATTENTION_COUNT,), 1.0, 3.0, (), jnp.float32)
    ridge_term = jnp.clip(jnp.exp(jax.random.uniform(splits[7], (ATTENTION_COUNT,), jnp.float32, math.log(0.5), math.log(2.0))), 0.5, 2.0)
    key_cache = scatter_about(splits[8], (PAGES, PAGE, ATTENTION_COUNT * DH), (DH ** -0.5), 1.25, ((0, 512),))
    value_cache = scatter_about(splits[9], (PAGES, PAGE, ATTENTION_COUNT * DH), 1.0, 6.0, ((0, 512),))
    log_weight = draw_log_weight(jax.random.fold_in(splits[18], 71), 0)
    page_owner = draw_page_owner(jax.random.fold_in(splits[18], 71), 0)
    page_fill = draw_page_fill(jax.random.fold_in(splits[18], 71), 0)
    out_weight = scatter_about(splits[13], (ATTENTION_COUNT * DH, D), (ATTENTION_COUNT * DH) ** -0.5, 0.1875, ((0, 16),))
    mlp_gain = jnp.clip(1.0 + 0.1 * jax.random.normal(splits[14], (D,), jnp.float32), 0.5, 1.5)
    gate_weight = scatter_about(splits[15], (D, FF), D ** -0.5, 0.1875, ((1, 16),))
    up_weight = scatter_about(splits[16], (D, FF), D ** -0.5, 0.1875, ((1, 16),))
    down_weight = scatter_about(splits[17], (FF, D), FF ** -0.5, 0.109375, ((0, 16),))
    return dict(tokens=tokens, norm_gain=norm_gain, qkv_weight=qkv_weight, conv_weight=conv_weight, conv_state=conv_state, mesa_gates=mesa_gates, mesa_bias=mesa_bias, ridge_term=ridge_term, key_cache=key_cache, value_cache=value_cache, log_weight=log_weight, page_owner=page_owner, page_fill=page_fill, out_weight=out_weight, mlp_gain=mlp_gain, gate_weight=gate_weight, up_weight=up_weight, down_weight=down_weight)


precise = lax.Precision.HIGHEST

def scaled_norm(row_vals, gain_vec):
    wide_rows = row_vals.astype(jnp.float32)
    factor = lax.rsqrt(lax.optimization_barrier(jnp.mean(wide_rows * wide_rows, axis=-1, keepdims=True)) + 1e-05)
    return (wide_rows * factor * gain_vec).astype(jnp.bfloat16)

def unit_rows(vectors):
    return vectors * lax.rsqrt(lax.optimization_barrier(jnp.sum(vectors * vectors, axis=-1, keepdims=True)) + 1e-06)

def slot_weights(owner_hot, decay_rows, log_weight, page_fill):
    page_len = log_weight.shape[2]
    slot_decay = jnp.dot(owner_hot, decay_rows, precision=precise)
    live_mask = (jnp.arange(page_len)[None, :] < page_fill[:, None]).astype(jnp.float32)
    return slot_decay[:, :, None] * jnp.exp(log_weight.astype(jnp.float32)) * live_mask[:, None, :]

def slot_terms(key_rows, source_rows, owner_hot, slot_weight, directions):
    slot_count, page_len, width_all = key_rows.shape
    head_count = slot_weight.shape[1]
    head_size = width_all // head_count
    member_count = owner_hot.shape[1]
    slot_dir = jnp.dot(owner_hot, directions.reshape(member_count, width_all), precision=precise)
    slot_dir = slot_dir.reshape(slot_count, head_count, head_size)
    key_wide = key_rows.astype(jnp.float32).reshape(slot_count, page_len, head_count, head_size)
    scores = jnp.einsum('sthd,shd->sht', key_wide, slot_dir, precision=precise)
    source_wide = source_rows.astype(jnp.float32).reshape(slot_count, page_len, head_count, head_size)
    contribution = jnp.einsum('sht,sthd->shd', slot_weight * scores, source_wide, precision=precise)
    summed = jnp.dot(owner_hot.T, contribution.reshape(slot_count, width_all), precision=precise)
    return summed.reshape(member_count, head_count, head_size)

def new_term(vectors, source_rows, strength_rows, key_new):
    return strength_rows[:, :, None] * source_rows * lax.optimization_barrier(jnp.sum(key_new * vectors, axis=-1, keepdims=True))

def conjugate(query_rows, key_new, value_new, strength_rows, ridge_term, reduce_fn):
    solution = jnp.zeros_like(query_rows)
    residual = query_rows
    direction = query_rows
    res_norm = lax.optimization_barrier(jnp.sum(residual * residual, axis=-1))
    for iteration in range(ITERS):
        image_vec = reduce_fn(direction, False) + new_term(direction, key_new, strength_rows, key_new) + ridge_term[None, :, None] * direction
        step_size = res_norm / lax.optimization_barrier(jnp.sum(direction * image_vec, axis=-1))
        solution = solution + step_size[:, :, None] * direction
        residual = residual - step_size[:, :, None] * image_vec
        next_norm = lax.optimization_barrier(jnp.sum(residual * residual, axis=-1))
        direction = residual + (next_norm / res_norm)[:, :, None] * direction
        res_norm = next_norm
    return reduce_fn(solution, True) + new_term(solution, value_new, strength_rows, key_new)

def reference(tokens, norm_gain, qkv_weight, conv_weight, conv_state, mesa_gates, mesa_bias, ridge_term, key_cache, value_cache, log_weight, page_owner, page_fill, out_weight, mlp_gain, gate_weight, up_weight, down_weight):
    row_count = tokens.shape[0]
    normed = scaled_norm(tokens, norm_gain)
    fresh_proj = jnp.dot(normed, qkv_weight, preferred_element_type=jnp.float32)
    past_rows = conv_state.astype(jnp.float32)
    pre_conv = conv_weight[3] * fresh_proj + conv_weight[0] * past_rows[:, 0] + conv_weight[1] * past_rows[:, 1] + conv_weight[2] * past_rows[:, 2]
    mixed_rows = jax.nn.silu(pre_conv).astype(jnp.bfloat16)
    split_rows = mixed_rows.astype(jnp.float32).reshape(row_count, 3, ATTENTION_COUNT, DH)
    query_rows = unit_rows(split_rows[:, 0])
    key_new = unit_rows(split_rows[:, 1])
    value_new = split_rows[:, 2]
    gate_vals = jax.nn.sigmoid(jnp.dot(normed, mesa_gates, preferred_element_type=jnp.float32) + mesa_bias)
    decay_rows = gate_vals[:, :ATTENTION_COUNT]
    strength_rows = gate_vals[:, ATTENTION_COUNT:]
    couple_number = N_GROUP // 2

    def per_pair(block):
        query_pair, key_pair, value_pair, decay_pair, strength_pair, keys_pair, values_pair, logw_pair, owner_pair, fill_pair = block
        owner_hot = (owner_pair[:, None] == jnp.arange(COUPLED_QUERIES)[None, :]).astype(jnp.float32)
        weights_pair = slot_weights(owner_hot, decay_pair, logw_pair, fill_pair)

        def reduce_fn(vectors, with_values):
            source_rows = values_pair if with_values else keys_pair
            return slot_terms(keys_pair, source_rows, owner_hot, weights_pair, vectors)
        return conjugate(query_pair, key_pair, value_pair, strength_pair, ridge_term, reduce_fn)
    blocks = (query_rows.reshape(couple_number, COUPLED_QUERIES, ATTENTION_COUNT, DH), key_new.reshape(couple_number, COUPLED_QUERIES, ATTENTION_COUNT, DH), value_new.reshape(couple_number, COUPLED_QUERIES, ATTENTION_COUNT, DH), decay_rows.reshape(couple_number, COUPLED_QUERIES, ATTENTION_COUNT), strength_rows.reshape(couple_number, COUPLED_QUERIES, ATTENTION_COUNT), key_cache.reshape(couple_number, SLOTS_PAIR, PAGE, ATTENTION_COUNT * DH), value_cache.reshape(couple_number, SLOTS_PAIR, PAGE, ATTENTION_COUNT * DH), log_weight.reshape(couple_number, SLOTS_PAIR, ATTENTION_COUNT, PAGE), page_owner.reshape(couple_number, SLOTS_PAIR), page_fill.reshape(couple_number, SLOTS_PAIR))
    found = lax.map(per_pair, blocks)
    retrieved = found.reshape(row_count, ATTENTION_COUNT * DH).astype(jnp.bfloat16)
    attended = jnp.dot(retrieved, out_weight, preferred_element_type=jnp.float32)
    mid_rows = (tokens.astype(jnp.float32) + attended).astype(jnp.bfloat16)
    mlp_in = scaled_norm(mid_rows, mlp_gain)
    gate_part = jnp.dot(mlp_in, gate_weight, preferred_element_type=jnp.float32)
    up_part = jnp.dot(mlp_in, up_weight, preferred_element_type=jnp.float32)
    hidden_rows = (jax.nn.silu(gate_part) * up_part).astype(jnp.bfloat16)
    down_part = jnp.dot(hidden_rows, down_weight, preferred_element_type=jnp.float32)
    layer_out = (mid_rows.astype(jnp.float32) + down_part).astype(jnp.bfloat16)
    return (retrieved, layer_out)
```

```python
import functools

import jax
import jax.numpy as jnp
from jax import lax
from jax.experimental import pallas as pl
from jax.experimental.pallas import tpu as pltpu
from jax.sharding import PartitionSpec as P

MESH = pl.DeviceIdType.MESH
F32 = jnp.float32
BF16 = jnp.bfloat16
ITERS = 4


def iota(shape, dim):
    return lax.broadcasted_iota(jnp.int32, shape, dim)


def mm(a, b):
    return jnp.dot(a, b, preferred_element_type=F32)


def mm_nt(a, b):
    return lax.dot_general(a, b, (((1,), (1,)), ((), ())), preferred_element_type=F32)


def split(v):
    hi = v.astype(BF16)
    lo = (v - hi.astype(F32)).astype(BF16)
    return hi, lo


def silu(v):
    return v / (1.0 + jnp.exp(-v))


def row_norm(wide, gain):
    factor = lax.rsqrt(jnp.mean(wide * wide, axis=-1, keepdims=True) + 1e-05)
    return (wide * factor * gain).astype(BF16)


def unit_rows(v):
    return v * lax.rsqrt(jnp.sum(v * v, axis=-1, keepdims=True) + 1e-06)


def rowsum(v):
    return jnp.sum(v, axis=-1, keepdims=True)


def kernel(
    tok_ref, ngain_ref, qkvw_hbm, convw_ref, convs_hbm, mgate_ref, mbias_ref, ridge_ref,
    key_hbm, val_hbm, logw_ref, owner_ref, fill_ref, outw_hbm, mgain_ref, gatew_hbm, upw_hbm, downw_hbm,
    ret_ref, lay_ref,
    qkvw, convs, outw, gatew, upw, downw,
    kall, vall, tokall, xrows, wo_src, wo_all, wmask,
    usrc, uall, gall, ohd, ohall, ohs,
    csrc, call, fsrc, fall, psrc, hall, msrc, mall, nsrc, nall,
    lsem, osem, ssem, rsem,
):
    g = lax.axis_index("group")
    s = lax.axis_index("shard")
    par = g % 2
    base = g - par
    y = s // 2
    c = s % 2
    q = par * 2 + c

    def local(src, dst, sem):
        cp = pltpu.make_async_copy(src, dst, sem)
        cp.start()
        return cp

    def remote(src, dst, send, recv, dev):
        pltpu.make_async_remote_copy(
            src_ref=src, dst_ref=dst, send_sem=send, recv_sem=recv,
            device_id=dev, device_id_type=MESH,
        ).start()

    def done(ref, sem):
        pltpu.make_async_copy(ref, ref, sem).wait()

    def each(n, fn):
        def step(k, carry):
            fn(k)
            return carry
        lax.fori_loop(0, n, step, 0)

    def team(t):
        return base + t // 2, 2 * y + t % 2

    def line(k):
        return g, 2 * ((y + k) % 8) + c

    bar = pltpu.get_barrier_semaphore()
    rank = par * 16 + s

    def greet(k):
        to = (rank + k + 1) % 32
        pl.semaphore_signal(bar, inc=1, device_id=(base + to // 16, to % 16), device_id_type=MESH)

    each(31, greet)

    c_conv = local(convs_hbm, convs, lsem.at[0])
    c_qkv = local(qkvw_hbm, qkvw, lsem.at[1])
    mine = pl.ds(pl.multiple_of(q * 256, 256), 256)
    local(key_hbm.at[:, :, mine], kall.at[pl.ds(q * 4, 4)], rsem.at[0])
    c_gate = local(gatew_hbm, gatew, lsem.at[2])
    c_up = local(upw_hbm, upw, lsem.at[3])
    c_down = local(downw_hbm, downw, lsem.at[4])
    local(outw_hbm, outw.at[c], rsem.at[1])
    local(val_hbm.at[:, :, mine], vall.at[pl.ds(q * 4, 4)], rsem.at[2])
    local(tok_ref, tokall.at[s], rsem.at[3])

    row8 = iota((8, 128), 0)
    lane8 = iota((8, 128), 1)
    slot8 = row8 % 4

    def pick(ref):
        return jnp.where(
            slot8 == 0, ref[0], jnp.where(slot8 == 1, ref[1], jnp.where(slot8 == 2, ref[2], ref[3]))
        )

    live = lane8 < pick(fill_ref)
    own8 = pick(owner_ref).astype(F32)
    logw = logw_ref[...].astype(F32)
    for t in range(4):
        rows = [logw[j, 2 * t + h : 2 * t + h + 1, :] for h in range(2) for j in range(4)]
        wo_src[t, 0:8, :] = jnp.where(live, jnp.exp(jnp.concatenate(rows, axis=0)), 0.0)
        wo_src[t, 8:16, :] = own8
    c_conv.wait()
    past = jnp.zeros((32, 192), F32)
    for k in range(3):
        past = past + convw_ref[k : k + 1, :] * convs[k].astype(F32)

    pl.semaphore_wait(bar, 31)

    def send_tok(k):
        to = (s + k + 1) % 16
        remote(tok_ref, tokall.at[s], ssem.at[0], rsem.at[3], (g, to))

    each(15, send_tok)
    local(wo_src.at[q], wo_all.at[q], rsem.at[4])

    def send_wo(k):
        t = (q + k + 1) % 4
        remote(wo_src.at[t], wo_all.at[q], ssem.at[1], rsem.at[4], team(t))

    each(3, send_wo)

    def send_key(k):
        t = (q + k + 1) % 4
        cols = pl.ds(pl.multiple_of(t * 256, 256), 256)
        remote(key_hbm.at[:, :, cols], kall.at[pl.ds(q * 4, 4)], ssem.at[2], rsem.at[0], team(t))

    each(3, send_key)

    c_qkv.wait()
    done(tokall, rsem.at[3])
    for i in range(16):
        xrows[2 * i : 2 * i + 2, :] = tokall[i].astype(F32)
    normed = row_norm(xrows[...], ngain_ref[...])
    fresh = mm(normed, qkvw[...])
    pre = convw_ref[3:4, :] * fresh + past
    mixed = silu(pre).astype(BF16).astype(F32)
    lane16 = iota((16, 128), 1)
    low16 = lane16 < 64
    a = mixed[:, 0:128]
    b = mixed[:, 64:192]

    def fold(lower, upper):
        return jnp.where(low16, lower, upper).astype(BF16)

    usrc[0] = fold(a[0:16], pltpu.roll(a[16:32], 64, 1))
    usrc[1] = fold(pltpu.roll(a[0:16], 64, 1), a[16:32])
    usrc[2] = fold(pltpu.roll(b[0:16], 64, 1), b[16:32])
    for j in range(3):
        unit = 3 * s + j
        part = unit % 16
        tq = part // 4
        slot = par * 12 + (unit // 16) * 4 + part % 4
        tg = base + tq // 2

        def send_unit(k, j=j, tq=tq, slot=slot, tg=tg):
            to = 2 * ((y + k + 1) % 8) + tq % 2
            remote(usrc.at[j], uall.at[slot], ssem.at[3], rsem.at[5], (tg, to))

        each(7, send_unit)

        @pl.when(tq == q)
        def _(j=j, slot=slot):
            local(usrc.at[j], uall.at[slot], rsem.at[5])

        @pl.when(tq != q)
        def _(j=j, slot=slot, tg=tg, tq=tq):
            remote(usrc.at[j], uall.at[slot], osem.at[j], rsem.at[5], (tg, 2 * y + tq % 2))

    gates = jax.nn.sigmoid(mm(normed, mgate_ref[...]) + mbias_ref[...])
    gall[par, :, 0:16] = gates
    remote(gall.at[par], gall.at[par], ssem.at[4], rsem.at[6], (base + 1 - par, s))

    done(wo_all, rsem.at[4])
    row32 = iota((32, 128), 0)
    lane32 = iota((32, 128), 1)
    first = (row32 // 4) % 2 == 0
    own32 = wo_all[:, 8:16, :].reshape(32, 128)
    hot = (own32 == (lane32 % 64).astype(F32)) & ((row32 // 4) % 2 == lane32 // 64)
    ohd[...] = hot.astype(F32).astype(BF16)
    local(ohd, ohall.at[y], rsem.at[7])

    def send_oh(k):
        remote(ohd, ohall.at[y], ssem.at[5], rsem.at[7], line(k + 1))

    each(7, send_oh)
    w32 = wo_all[:, 0:8, :].reshape(32, 128)
    slot32 = (row32 // 8) * 4 + row32 % 4
    for p in range(16):
        wmask[:, 128 * p : 128 * p + 128] = jnp.where(slot32 == p, w32, 0.0)

    done(uall, rsem.at[5])
    done(gall.at[0], rsem.at[6])

    def send_val(k):
        t = (q + k + 1) % 4
        cols = pl.ds(pl.multiple_of(t * 256, 256), 256)
        remote(val_hbm.at[:, :, cols], vall.at[pl.ds(q * 4, 4)], ssem.at[6], rsem.at[2], team(t))

    each(3, send_val)
    remote(outw_hbm, outw.at[c], ssem.at[7], rsem.at[1], (g, 2 * y + 1 - c))

    def unfold(kind):
        blocks = []
        for h in range(2):
            for p in range(2):
                left = uall[p * 12 + kind * 4 + 2 * h].astype(F32)
                right = uall[p * 12 + kind * 4 + 2 * h + 1].astype(F32)
                blocks.append(jnp.where(low16, left, pltpu.roll(right, 64, 1)))
                blocks.append(jnp.where(low16, pltpu.roll(left, 64, 1), right))
        return jnp.concatenate(blocks, axis=0)

    query = unit_rows(unfold(0))
    knew = unit_rows(unfold(1))
    vnew = unfold(2)
    gboth = gall[...].reshape(64, 128)
    lane64 = iota((64, 128), 1)

    def column(at):
        halves = [rowsum(jnp.where(lane64 == at + h, gboth, 0.0)) for h in range(2)]
        return jnp.concatenate(halves, axis=0)

    decay = column(2 * q)
    strength = column(8 + 2 * q)
    rowc = iota((128, 1), 0)
    ridge = jnp.where(rowc < 64, ridge_ref[2 * q], ridge_ref[2 * q + 1])

    done(ohall, rsem.at[7])
    ohs[...] = ohall[...].reshape(256, 128).astype(F32).T.astype(BF16)
    done(kall, rsem.at[0])

    def spread(picked):
        return jnp.concatenate([jnp.where(first, picked, 0.0), jnp.where(first, 0.0, picked)], axis=1)

    def weigh(scores):
        hi, lo = split((scores[0:32] + scores[32:64]) * wmask[...])
        return jnp.concatenate([hi, lo], axis=0)

    def gathered(prod):
        both = prod[0:32] + prod[32:64]
        return jnp.where(first, both[:, 0:128], both[:, 128:256])

    def own_term(vec, source):
        return strength * source * rowsum(knew * vec)

    keys = kall[...].reshape(2048, 256)
    solution = jnp.zeros((128, 128), F32)
    residual = query
    direction = query
    res_norm = rowsum(residual * residual)
    for it in range(ITERS - 1):
        hi, lo = split(direction)
        sel = mm(ohd[...], jnp.concatenate([hi, lo], axis=1))
        lhs = jnp.concatenate([spread(sel[:, 0:128]), spread(sel[:, 128:256])], axis=0).astype(BF16)
        csrc[it] = gathered(mm(weigh(mm_nt(lhs, keys)), keys)).astype(BF16)
        local(csrc.at[it], call.at[it, y], rsem.at[8 + it])

        def send_c(k, it=it):
            remote(csrc.at[it], call.at[it, y], ssem.at[8 + it], rsem.at[8 + it], line(k + 1))

        each(7, send_c)
        near = own_term(direction, knew) + ridge * direction
        done(call.at[it], rsem.at[8 + it])
        image = decay * mm(ohs[...], call[it].reshape(256, 128)) + near
        step_size = res_norm / rowsum(direction * image)
        solution = solution + step_size * direction
        residual = residual - step_size * image
        next_norm = rowsum(residual * residual)
        direction = residual + (next_norm / res_norm) * direction
        res_norm = next_norm

    dhi, dlo = split(direction)
    xhi, xlo = split(solution)
    sel = mm(ohd[...], jnp.concatenate([dhi, dlo, xhi, xlo], axis=1))
    lhs = jnp.concatenate([spread(sel[:, 128 * i : 128 * i + 128]) for i in range(4)], axis=0).astype(BF16)
    scores = mm_nt(lhs, keys)
    dweigh = weigh(scores[0:64])
    xweigh = weigh(scores[64:128])
    fsrc[0:32, :] = gathered(mm(dweigh, keys)).astype(BF16)
    done(vall, rsem.at[2])
    values = vall[...].reshape(2048, 256)
    reads = mm(jnp.concatenate([dweigh, xweigh], axis=0), values)
    fsrc[32:64, :] = gathered(reads[0:64]).astype(BF16)
    fsrc[64:96, :] = gathered(reads[64:128]).astype(BF16)
    active = q == y // 2
    for h in range(2):
        ty = 2 * q + h

        @pl.when(ty == y)
        def _():
            local(fsrc, fall.at[y], rsem.at[11])

        @pl.when(ty != y)
        def _(h=h, ty=ty):
            remote(fsrc, fall.at[y], osem.at[3 + h], rsem.at[11], (g, 2 * ty + c))

    done(outw, rsem.at[1])

    @pl.when(active)
    def _():
        near = own_term(direction, knew) + ridge * direction
        near_d = own_term(direction, vnew)
        near_x = own_term(solution, vnew)
        done(fall, rsem.at[11])
        got = [mm(ohs[...], fall[:, 32 * i : 32 * i + 32, :].reshape(256, 128)) for i in range(3)]
        image = decay * got[0] + near
        step_size = res_norm / rowsum(direction * image)
        both = decay * got[2] + near_x + step_size * (decay * got[1] + near_d)
        found = jnp.where(y % 2 == 0, both[0:64], both[64:128]).astype(BF16)
        partial = mm(found, outw[...].reshape(128, 1024)).astype(BF16)
        for r in range(32):
            psrc[r, :, 0:1024] = partial[2 * r : 2 * r + 2, :]
            psrc[r, :, 1024:1152] = found[2 * r : 2 * r + 2, :]
        local(psrc.at[rank], hall.at[y], rsem.at[12])

        def send_p(k):
            to = (rank + k + 1) % 32
            remote(psrc.at[to], hall.at[y], ssem.at[11], rsem.at[12], (base + to // 16, to % 16))

        each(31, send_p)

    done(hall, rsem.at[12])
    attended = jnp.zeros((2, 1024), F32)
    for h in range(8):
        attended = attended + hall[h, :, 0:1024].astype(F32)
        ret_ref[:, 128 * h : 128 * h + 128] = hall[h, :, 1024:1152]
    mid = (tok_ref[...].astype(F32) + attended).astype(BF16).astype(F32)
    msrc[...] = row_norm(mid, mgain_ref[...])
    local(msrc, mall.at[s], rsem.at[13])

    def send_m(k):
        remote(msrc, mall.at[s], ssem.at[12], rsem.at[13], (g, (s + k + 1) % 16))

    each(15, send_m)
    c_gate.wait()
    c_up.wait()
    c_down.wait()
    done(mall, rsem.at[13])
    for i in range(16):
        xrows[2 * i : 2 * i + 2, :] = mall[i].astype(F32)
    rows = xrows[...].astype(BF16)
    hidden = (silu(mm(rows, gatew[...])) * mm(rows, upw[...])).astype(BF16)
    down = mm(hidden, downw[...]).astype(BF16)
    for r in range(16):
        nsrc[r] = down[2 * r : 2 * r + 2, :]
    local(nsrc.at[s], nall.at[s], rsem.at[14])

    def send_n(k):
        to = (s + k + 1) % 16
        remote(nsrc.at[to], nall.at[s], ssem.at[13], rsem.at[14], (g, to))

    each(15, send_n)
    done(nall, rsem.at[14])
    total = mid
    for i in range(16):
        total = total + nall[i].astype(F32)
    lay_ref[...] = total.astype(BF16)

    done(tokall.at[pl.ds(0, 15)], ssem.at[0])
    done(wo_all.at[pl.ds(0, 3)], ssem.at[1])
    done(kall.at[pl.ds(0, 12)], ssem.at[2])
    done(uall.at[pl.ds(0, 21)], ssem.at[3])
    done(gall.at[0], ssem.at[4])
    done(ohall.at[pl.ds(0, 7)], ssem.at[5])
    done(vall.at[pl.ds(0, 12)], ssem.at[6])
    done(outw.at[0], ssem.at[7])
    for it in range(ITERS - 1):
        done(call.at[it, pl.ds(0, 7)], ssem.at[8 + it])
    for j in range(3):
        @pl.when(((3 * s + j) % 16) // 4 != q)
        def _(j=j):
            done(usrc.at[j], osem.at[j])
    for h in range(2):
        @pl.when(2 * q + h != y)
        def _(h=h):
            done(fsrc, osem.at[3 + h])

    @pl.when(active)
    def _():
        done(psrc.at[pl.ds(0, 31)], ssem.at[11])

    @pl.when(jnp.logical_not(active))
    def _():
        pass

    done(mall.at[pl.ds(0, 15)], ssem.at[12])
    done(nall.at[pl.ds(0, 15)], ssem.at[13])


def body(
    tokens, norm_gain, qkv_weight, conv_weight, conv_state, mesa_gates, mesa_bias, ridge_term,
    key_cache, value_cache, log_weight, page_owner, page_fill, out_weight, mlp_gain,
    gate_weight, up_weight, down_weight,
):
    vm = pl.BlockSpec(memory_space=pltpu.VMEM)
    sm = pl.BlockSpec(memory_space=pltpu.SMEM)
    hb = pl.BlockSpec(memory_space=pltpu.HBM)
    v = pltpu.VMEM
    dma = pltpu.SemaphoreType.DMA
    return pl.pallas_call(
        kernel,
        name="layer",
        out_shape=(
            jax.ShapeDtypeStruct((2, 1024), BF16),
            jax.ShapeDtypeStruct((2, 1024), BF16),
        ),
        in_specs=[vm, vm, hb, vm, hb, vm, vm, sm, hb, hb, vm, sm, sm, hb, vm, hb, hb, hb],
        out_specs=(vm, vm),
        scratch_shapes=[
            v((1024, 192), BF16), v((3, 32, 192), BF16), v((2, 64, 1024), BF16),
            v((1024, 176), BF16), v((1024, 176), BF16), v((176, 1024), BF16),
            v((16, 128, 256), BF16), v((16, 128, 256), BF16),
            v((16, 2, 1024), BF16), v((32, 1024), F32),
            v((4, 16, 128), F32), v((4, 16, 128), F32), v((32, 2048), F32),
            v((3, 16, 128), BF16), v((24, 16, 128), BF16), v((2, 32, 128), F32),
            v((32, 128), BF16), v((8, 32, 128), BF16), v((128, 256), BF16),
            v((3, 32, 128), BF16), v((3, 8, 32, 128), BF16),
            v((96, 128), BF16), v((8, 96, 128), BF16),
            v((32, 2, 1152), BF16), v((8, 2, 1152), BF16),
            v((2, 1024), BF16), v((16, 2, 1024), BF16),
            v((16, 2, 1024), BF16), v((16, 2, 1024), BF16),
            dma((5,)), dma((5,)), dma((14,)), dma((15,)),
        ],
        compiler_params=pltpu.CompilerParams(
            collective_id=0, has_side_effects=True, vmem_limit_bytes=56 * 1024 * 1024
        ),
    )(
        tokens, norm_gain.reshape(1, -1), qkv_weight, conv_weight, conv_state.transpose(1, 0, 2),
        mesa_gates, mesa_bias.reshape(1, -1), ridge_term, key_cache, value_cache, log_weight,
        page_owner, page_fill, out_weight, mlp_gain.reshape(1, -1), gate_weight, up_weight, down_weight,
    )


def solution(mesh):
    return jax.shard_map(
        body,
        mesh=mesh,
        in_specs=(
            P(("group", "shard"), None),
            P(),
            P(None, "shard"),
            P(None, "shard"),
            P("group", None, "shard"),
            P(),
            P(),
            P(),
            P(("group", "shard"), None, None),
            P(("group", "shard"), None, None),
            P(("group", "shard"), None, None),
            P(("group", "shard")),
            P(("group", "shard")),
            P("shard", None),
            P(),
            P(None, "shard"),
            P(None, "shard"),
            P("shard", None),
        ),
        out_specs=(P(("group", "shard"), None), P(("group", "shard"), None)),
        check_vma=False,
    )
```

```python
import functools

import jax
import jax.numpy as jnp
from jax import lax
from jax.experimental import pallas as pl
from jax.experimental.pallas import tpu as pltpu
from jax.sharding import PartitionSpec as P

MESH = pl.DeviceIdType.MESH
F32 = jnp.float32
BF16 = jnp.bfloat16
ITERS = 4


def iota(shape, dim):
    return lax.broadcasted_iota(jnp.int32, shape, dim)


def mm(a, b):
    return jnp.dot(a, b, preferred_element_type=F32)


def mm_nt(a, b):
    return lax.dot_general(a, b, (((1,), (1,)), ((), ())), preferred_element_type=F32)


def split(v):
    hi = v.astype(BF16)
    lo = (v - hi.astype(F32)).astype(BF16)
    return hi, lo


def silu(v):
    return v / (1.0 + jnp.exp(-v))


def row_norm(wide, gain):
    factor = lax.rsqrt(jnp.mean(wide * wide, axis=-1, keepdims=True) + 1e-05)
    return (wide * factor * gain).astype(BF16)


def unit_rows(v):
    return v * lax.rsqrt(jnp.sum(v * v, axis=-1, keepdims=True) + 1e-06)


def rowsum(v):
    return jnp.sum(v, axis=-1, keepdims=True)


def kernel(
    tok_ref, ngain_ref, qkvw_hbm, convw_ref, convs_hbm, mgate_ref, mbias_ref, ridge_ref,
    key_hbm, val_hbm, logw_ref, owner_ref, fill_ref, outw_hbm, mgain_ref, gatew_hbm, upw_hbm, downw_hbm,
    ret_ref, lay_ref,
    qkvw, convs, outw, gatew, upw, downw,
    kall, vall, tokall, xrows, wo_src, wo_all, wmask,
    usrc, uall, gall, ohd, ohall, ohs,
    csrc, call, rsrc, rall, fsrc, fall, tsrc, tall, nsrc, nall,
    lsem, osem, ssem, rsem,
):
    g = lax.axis_index("group")
    s = lax.axis_index("shard")
    par = g % 2
    base = g - par
    y = s // 2
    c = s % 2
    q = par * 2 + c

    def local(src, dst, sem):
        cp = pltpu.make_async_copy(src, dst, sem)
        cp.start()
        return cp

    def remote(src, dst, send, recv, dev):
        pltpu.make_async_remote_copy(
            src_ref=src, dst_ref=dst, send_sem=send, recv_sem=recv,
            device_id=dev, device_id_type=MESH,
        ).start()

    def done(ref, sem):
        pltpu.make_async_copy(ref, ref, sem).wait()

    def each(n, fn):
        def step(k, carry):
            fn(k)
            return carry
        lax.fori_loop(0, n, step, 0)

    def team(t):
        return base + t // 2, 2 * y + t % 2

    def line(k):
        return g, 2 * ((y + k) % 8) + c

    def pass_on(k):
        if k > 1:
            done(outw.at[pl.ds(0, 2), 0], rsem.at[16 + k])
        low, high = (y + 9 - k) % 8, (y + k - 1) % 8
        for way, at, to in ((0, low, 1), (1, high, 7)):
            rows = pl.ds(32 * way, 32) if k == 4 else pl.ds(0, 64)
            src = outw_hbm if k == 1 else outw.at[at, c, rows]
            remote(src, outw.at[at, c, rows], ssem.at[15 + k], rsem.at[17 + k], line(to))

    bar = pltpu.get_barrier_semaphore()
    rank = par * 16 + s

    def greet(k):
        to = (rank + k + 1) % 32
        pl.semaphore_signal(bar, inc=1, device_id=(base + to // 16, to % 16), device_id_type=MESH)

    each(31, greet)

    c_conv = local(convs_hbm, convs, lsem.at[0])
    c_qkv = local(qkvw_hbm, qkvw, lsem.at[1])
    mine = pl.ds(pl.multiple_of(q * 256, 256), 256)
    local(key_hbm.at[:, :, mine], kall.at[pl.ds(q * 4, 4)], rsem.at[0])
    c_gate = local(gatew_hbm, gatew, lsem.at[2])
    c_up = local(upw_hbm, upw, lsem.at[3])
    c_down = local(downw_hbm, downw, lsem.at[4])
    local(outw_hbm, outw.at[y, c], rsem.at[1])
    local(val_hbm.at[:, :, mine], vall.at[pl.ds(q * 4, 4)], rsem.at[2])
    local(tok_ref, tokall.at[s], rsem.at[3])

    row8 = iota((8, 128), 0)
    lane8 = iota((8, 128), 1)
    slot8 = row8 % 4

    def pick(ref):
        return jnp.where(
            slot8 == 0, ref[0], jnp.where(slot8 == 1, ref[1], jnp.where(slot8 == 2, ref[2], ref[3]))
        )

    live = lane8 < pick(fill_ref)
    own8 = pick(owner_ref).astype(F32)
    logw = logw_ref[...].astype(F32)
    for t in range(4):
        rows = [logw[j, 2 * t + h : 2 * t + h + 1, :] for h in range(2) for j in range(4)]
        wo_src[t, 0:8, :] = jnp.where(live, jnp.exp(jnp.concatenate(rows, axis=0)), 0.0)
        wo_src[t, 8:16, :] = own8
    c_conv.wait()
    past = jnp.zeros((32, 192), F32)
    for k in range(3):
        past = past + convw_ref[k : k + 1, :] * convs[k].astype(F32)

    pl.semaphore_wait(bar, 31)

    def send_tok(k):
        to = (s + k + 1) % 16
        remote(tok_ref, tokall.at[s], ssem.at[0], rsem.at[3], (g, to))

    each(15, send_tok)
    local(wo_src.at[q], wo_all.at[q], rsem.at[4])

    def send_wo(k):
        t = (q + k + 1) % 4
        remote(wo_src.at[t], wo_all.at[q], ssem.at[1], rsem.at[4], team(t))

    each(3, send_wo)

    def send_key(k):
        t = (q + k + 1) % 4
        cols = pl.ds(pl.multiple_of(t * 256, 256), 256)
        remote(key_hbm.at[:, :, cols], kall.at[pl.ds(q * 4, 4)], ssem.at[2], rsem.at[0], team(t))

    each(3, send_key)
    pass_on(1)

    c_qkv.wait()
    done(tokall, rsem.at[3])
    for i in range(16):
        xrows[2 * i : 2 * i + 2, :] = tokall[i].astype(F32)
    normed = row_norm(xrows[...], ngain_ref[...])
    fresh = mm_nt(normed, qkvw[...])
    pre = convw_ref[3:4, :] * fresh + past
    mixed = silu(pre).astype(BF16).astype(F32)
    lane16 = iota((16, 128), 1)
    low16 = lane16 < 64
    a = mixed[:, 0:128]
    b = mixed[:, 64:192]

    def fold(lower, upper):
        return jnp.where(low16, lower, upper).astype(BF16)

    usrc[0] = fold(a[0:16], pltpu.roll(a[16:32], 64, 1))
    usrc[1] = fold(pltpu.roll(a[0:16], 64, 1), a[16:32])
    usrc[2] = fold(pltpu.roll(b[0:16], 64, 1), b[16:32])
    for j in range(3):
        unit = 3 * s + j
        part = unit % 16
        tq = part // 4
        kind = unit // 16
        slot = kind * 8 + par * 4 + part % 4
        got = rsem.at[13 + kind]
        tg = base + tq // 2

        def send_unit(k, j=j, tq=tq, slot=slot, tg=tg, got=got):
            to = 2 * ((y + k + 1) % 8) + tq % 2
            remote(usrc.at[j], uall.at[slot], ssem.at[3], got, (tg, to))

        each(7, send_unit)

        @pl.when(tq == q)
        def _(j=j, slot=slot, got=got):
            local(usrc.at[j], uall.at[slot], got)

        @pl.when(tq != q)
        def _(j=j, slot=slot, tg=tg, tq=tq, got=got):
            remote(usrc.at[j], uall.at[slot], osem.at[j], got, (tg, 2 * y + tq % 2))

    gates = jax.nn.sigmoid(mm_nt(normed, mgate_ref[...]) + mbias_ref[...])
    gall[par, :, 0:16] = gates
    remote(gall.at[par], gall.at[par], ssem.at[4], rsem.at[6], (base + 1 - par, s))

    done(wo_all, rsem.at[4])
    row32 = iota((32, 128), 0)
    lane32 = iota((32, 128), 1)
    first = (row32 // 4) % 2 == 0
    own32 = wo_all[:, 8:16, :].reshape(32, 128)
    hot = (own32 == (lane32 % 64).astype(F32)) & ((row32 // 4) % 2 == lane32 // 64)
    ohd[...] = hot.astype(F32).astype(BF16)
    local(ohd, ohall.at[y], rsem.at[7])

    def send_oh(k):
        remote(ohd, ohall.at[y], ssem.at[5], rsem.at[7], line(k + 1))

    each(7, send_oh)
    w32 = wo_all[:, 0:8, :].reshape(32, 128)
    slot32 = (row32 // 8) * 4 + row32 % 4
    for p in range(16):
        wmask[:, 128 * p : 128 * p + 128] = jnp.where(slot32 == p, w32, 0.0)

    def send_val(k):
        t = (q + k + 1) % 4
        cols = pl.ds(pl.multiple_of(t * 256, 256), 256)
        remote(val_hbm.at[:, :, cols], vall.at[pl.ds(q * 4, 4)], ssem.at[6], rsem.at[2], team(t))

    each(3, send_val)

    pass_on(2)

    def unfold(kind):
        blocks = []
        for h in range(2):
            for p in range(2):
                left = uall[kind * 8 + p * 4 + 2 * h].astype(F32)
                right = uall[kind * 8 + p * 4 + 2 * h + 1].astype(F32)
                blocks.append(jnp.where(low16, left, pltpu.roll(right, 64, 1)))
                blocks.append(jnp.where(low16, pltpu.roll(left, 64, 1), right))
        return jnp.concatenate(blocks, axis=0)

    done(uall.at[pl.ds(0, 8)], rsem.at[13])
    query = unit_rows(unfold(0))
    done(kall, rsem.at[0])

    def spread(picked):
        return jnp.concatenate([jnp.where(first, picked, 0.0), jnp.where(first, 0.0, picked)], axis=1)

    def slot_rows(vec):
        hi, lo = split(vec)
        sel = mm(ohd[...], jnp.concatenate([hi, lo], axis=1))
        return jnp.concatenate([spread(sel[:, 0:128]), spread(sel[:, 128:256])], axis=0).astype(BF16)

    def weigh(scores):
        hi, lo = split((scores[0:32] + scores[32:64]) * wmask[...])
        return jnp.concatenate([hi, lo], axis=0)

    def gathered(prod):
        both = prod[0:32] + prod[32:64]
        return jnp.where(first, both[:, 0:128], both[:, 128:256]).astype(BF16)

    def own_term(vec, source):
        return strength * source * rowsum(knew * vec)

    def summed(part):
        return decay * mm(ohs[...], part.reshape(256, 128))

    keys = kall[...].reshape(2048, 256)
    solution = jnp.zeros((128, 128), F32)
    residual = query
    direction = query
    res_norm = rowsum(residual * residual)
    for it in range(ITERS):
        last = it == ITERS - 1
        src, dst = (fsrc, fall) if last else (csrc.at[it], call.at[it])
        weighed = weigh(mm_nt(slot_rows(direction), keys))
        src[0:32, :] = gathered(mm(weighed, keys))
        if last:
            values = vall[...].reshape(2048, 256)
            src[32:64, :] = gathered(mm(weighed, values))
        local(src, dst.at[y], rsem.at[8 + it])

        def send_c(k, it=it, src=src, dst=dst):
            remote(src, dst.at[y], ssem.at[8 + it], rsem.at[8 + it], line(k + 1))

        each(7, send_c)
        if it == 0:
            done(uall.at[pl.ds(8, 8)], rsem.at[14])
            knew = unit_rows(unfold(1))
            done(gall.at[0], rsem.at[6])
            gboth = gall[...].reshape(64, 128)
            lane64 = iota((64, 128), 1)

            def column(at):
                halves = [rowsum(jnp.where(lane64 == at + h, gboth, 0.0)) for h in range(2)]
                return jnp.concatenate(halves, axis=0)

            decay = column(2 * q)
            strength = column(8 + 2 * q)
            rowc = iota((128, 1), 0)
            ridge = jnp.where(rowc < 64, ridge_ref[2 * q], ridge_ref[2 * q + 1])
            done(ohall, rsem.at[7])
            ohs[...] = ohall[...].reshape(256, 128).astype(F32).T.astype(BF16)
            pass_on(3)
        if it == 1:
            pass_on(4)
            done(uall.at[pl.ds(16, 8)], rsem.at[15])
            vnew = unfold(2)
        if it == ITERS - 2:
            done(vall, rsem.at[2])
            values = vall[...].reshape(2048, 256)
            xweighed = weigh(mm_nt(slot_rows(solution), keys))
            reads = mm(jnp.concatenate([weighed, xweighed], axis=0), values)
            rsrc[0:32, :] = gathered(reads[0:64])
            rsrc[32:64, :] = gathered(reads[64:128])
            local(rsrc, rall.at[y], rsem.at[12])

            def send_r(k):
                remote(rsrc, rall.at[y], ssem.at[12], rsem.at[12], line(k + 1))

            each(7, send_r)
            done(outw.at[0, 0], rsem.at[1])
            done(outw.at[0, 0], rsem.at[21])
            remote(outw.at[:, c], outw.at[:, c], ssem.at[13], rsem.at[5], (g, 2 * y + 1 - c))
        near = own_term(direction, knew) + ridge * direction
        if last:
            done(rall, rsem.at[12])
            read_x = summed(rall[:, 32:64, :]) + step_size * summed(rall[:, 0:32, :])
            near_d = own_term(direction, vnew)
            near_x = own_term(solution, vnew)
        done(dst, rsem.at[8 + it])
        image = summed(dst[:, 0:32, :]) + near
        step_size = res_norm / rowsum(direction * image)
        if not last:
            solution = solution + step_size * direction
            residual = residual - step_size * image
            next_norm = rowsum(residual * residual)
            direction = residual + (next_norm / res_norm) * direction
            res_norm = next_norm
    found = (read_x + near_x + step_size * (summed(fall[:, 32:64, :]) + near_d)).astype(BF16)

    for p in range(2):
        for h in range(2):
            tsrc[p, h] = found[64 * h + 32 * p : 64 * h + 32 * p + 32, :]
    local(tsrc.at[par], tall.at[q], rsem.at[16])

    def send_t(k):
        t = (q + k + 1) % 4
        remote(tsrc.at[t // 2], tall.at[q], ssem.at[14], rsem.at[16], team(t))

    each(3, send_t)
    done(outw.at[:, c], rsem.at[5])
    done(tall, rsem.at[16])
    heads = jnp.concatenate([tall[h // 2, h % 2] for h in range(8)], axis=1)
    attended = mm(heads, outw[...].reshape(1024, 1024))
    mid = (xrows[...] + attended).astype(BF16)
    rows = row_norm(mid.astype(F32), mgain_ref[...])
    c_gate.wait()
    c_up.wait()
    c_down.wait()
    hidden = (silu(mm_nt(rows, gatew[...])) * mm_nt(rows, upw[...])).astype(BF16)
    down = mm(hidden, downw[...]).astype(BF16)
    for r in range(16):
        nsrc[r] = down[2 * r : 2 * r + 2, :]
    local(nsrc.at[s], nall.at[s], rsem.at[17])

    def send_n(k):
        to = (s + k + 1) % 16
        remote(nsrc.at[to], nall.at[s], ssem.at[15], rsem.at[17], (g, to))

    each(15, send_n)
    mine8 = (iota((8, 32), 1) == 2 * s + iota((8, 32), 0)).astype(F32).astype(BF16)
    ret_ref[...] = mm(mine8, heads)[0:2].astype(BF16)
    total = mm(mine8, mid)[0:2]
    done(nall, rsem.at[17])
    for i in range(16):
        total = total + nall[i].astype(F32)
    lay_ref[...] = total.astype(BF16)

    done(tokall.at[pl.ds(0, 15)], ssem.at[0])
    done(wo_all.at[pl.ds(0, 3)], ssem.at[1])
    done(kall.at[pl.ds(0, 12)], ssem.at[2])
    done(uall.at[pl.ds(0, 21)], ssem.at[3])
    done(gall.at[0], ssem.at[4])
    done(ohall.at[pl.ds(0, 7)], ssem.at[5])
    done(vall.at[pl.ds(0, 12)], ssem.at[6])
    for k in range(1, 5):
        done(outw.at[pl.ds(0, 1 if k == 4 else 2), 0], ssem.at[15 + k])
    for it in range(ITERS - 1):
        done(call.at[it, pl.ds(0, 7)], ssem.at[8 + it])
    done(fall.at[pl.ds(0, 7)], ssem.at[11])
    done(rall.at[pl.ds(0, 7)], ssem.at[12])
    done(outw.at[:, 0], ssem.at[13])
    done(tall.at[pl.ds(0, 3)], ssem.at[14])
    done(nall.at[pl.ds(0, 15)], ssem.at[15])
    for j in range(3):
        @pl.when(((3 * s + j) % 16) // 4 != q)
        def _(j=j):
            done(usrc.at[j], osem.at[j])


def body(
    tokens, norm_gain, qkv_weight, conv_weight, conv_state, mesa_gates, mesa_bias, ridge_term,
    key_cache, value_cache, log_weight, page_owner, page_fill, out_weight, mlp_gain,
    gate_weight, up_weight, down_weight,
):
    vm = pl.BlockSpec(memory_space=pltpu.VMEM)
    sm = pl.BlockSpec(memory_space=pltpu.SMEM)
    hb = pl.BlockSpec(memory_space=pltpu.HBM)
    v = pltpu.VMEM
    dma = pltpu.SemaphoreType.DMA
    return pl.pallas_call(
        kernel,
        name="layer",
        out_shape=(
            jax.ShapeDtypeStruct((2, 1024), BF16),
            jax.ShapeDtypeStruct((2, 1024), BF16),
        ),
        in_specs=[vm, vm, hb, vm, hb, vm, vm, sm, hb, hb, vm, sm, sm, hb, vm, hb, hb, hb],
        out_specs=(vm, vm),
        scratch_shapes=[
            v((192, 1024), BF16), v((3, 32, 192), BF16), v((8, 2, 64, 1024), BF16),
            v((176, 1024), BF16), v((176, 1024), BF16), v((176, 1024), BF16),
            v((16, 128, 256), BF16), v((16, 128, 256), BF16),
            v((16, 2, 1024), BF16), v((32, 1024), F32),
            v((4, 16, 128), F32), v((4, 16, 128), F32), v((32, 2048), F32),
            v((3, 16, 128), BF16), v((24, 16, 128), BF16), v((2, 32, 128), F32),
            v((32, 128), BF16), v((8, 32, 128), BF16), v((128, 256), BF16),
            v((3, 32, 128), BF16), v((3, 8, 32, 128), BF16),
            v((64, 128), BF16), v((8, 64, 128), BF16),
            v((64, 128), BF16), v((8, 64, 128), BF16),
            v((2, 2, 32, 128), BF16), v((4, 2, 32, 128), BF16),
            v((16, 2, 1024), BF16), v((16, 2, 1024), BF16),
            dma((5,)), dma((3,)), dma((20,)), dma((22,)),
        ],
        compiler_params=pltpu.CompilerParams(
            collective_id=0, has_side_effects=True, vmem_limit_bytes=56 * 1024 * 1024
        ),
    )(
        tokens, norm_gain.reshape(1, -1), qkv_weight.T, conv_weight, conv_state.transpose(1, 0, 2),
        mesa_gates.T, mesa_bias.reshape(1, -1), ridge_term, key_cache, value_cache, log_weight,
        page_owner, page_fill, out_weight, mlp_gain.reshape(1, -1), gate_weight.T, up_weight.T, down_weight,
    )


def solution(mesh):
    return jax.shard_map(
        body,
        mesh=mesh,
        in_specs=(
            P(("group", "shard"), None),
            P(),
            P(None, "shard"),
            P(None, "shard"),
            P("group", None, "shard"),
            P(),
            P(),
            P(),
            P(("group", "shard"), None, None),
            P(("group", "shard"), None, None),
            P(("group", "shard"), None, None),
            P(("group", "shard")),
            P(("group", "shard")),
            P("shard", None),
            P(),
            P(None, "shard"),
            P(None, "shard"),
            P("shard", None),
        ),
        out_specs=(P(("group", "shard"), None), P(("group", "shard"), None)),
        check_vma=False,
    )
```

```python
import functools

import jax
import jax.numpy as jnp
from jax import lax
from jax.experimental import pallas as pl
from jax.experimental.pallas import tpu as pltpu
from jax.sharding import PartitionSpec as P

MESH = pl.DeviceIdType.MESH
F32 = jnp.float32
BF16 = jnp.bfloat16
ITERS = 4


def iota(shape, dim):
    return lax.broadcasted_iota(jnp.int32, shape, dim)


def mm(a, b):
    return jnp.dot(a, b, preferred_element_type=F32)


def mm_nt(a, b):
    return lax.dot_general(a, b, (((1,), (1,)), ((), ())), preferred_element_type=F32)


def split(v):
    hi = v.astype(BF16)
    lo = (v - hi.astype(F32)).astype(BF16)
    return hi, lo


def silu(v):
    return v / (1.0 + jnp.exp(-v))


def row_norm(wide, gain):
    factor = lax.rsqrt(jnp.mean(wide * wide, axis=-1, keepdims=True) + 1e-05)
    return (wide * factor * gain).astype(BF16)


def unit_rows(v):
    return v * lax.rsqrt(jnp.sum(v * v, axis=-1, keepdims=True) + 1e-06)


def rowsum(v):
    return jnp.sum(v, axis=-1, keepdims=True)


def kernel(
    tok_ref, ngain_ref, qkvw_hbm, convw_ref, convs_hbm, mgate_ref, mbias_ref, ridge_ref,
    key_hbm, val_hbm, logw_ref, owner_ref, fill_ref, outw_hbm, mgain_ref, gatew_hbm, upw_hbm, downw_hbm,
    ret_ref, lay_ref,
    qkvw, convs, outw, gatew, upw, downw,
    kall, vall, tokall, xrows, wo_src, wo_all, wmask, past_out, past_in,
    usrc, uall, gall, own_src, own_all, ohd, oht,
    csrc, call, rsrc, rall, fsrc, fall, tsrc, tall, nsrc, nall, hsrc, hall,
    kturn, lsem, osem, ssem, rsem,
):
    g = lax.axis_index("group")
    s = lax.axis_index("shard")
    par = g % 2
    base = g - par
    y = s // 2
    c = s % 2
    q = par * 2 + c
    partner = base + 1 - par

    def local(src, dst, sem):
        cp = pltpu.make_async_copy(src, dst, sem)
        cp.start()
        return cp

    def remote(src, dst, send, recv, dev):
        pltpu.make_async_remote_copy(
            src_ref=src, dst_ref=dst, send_sem=send, recv_sem=recv,
            device_id=dev, device_id_type=MESH,
        ).start()

    def done(ref, sem):
        pltpu.make_async_copy(ref, ref, sem).wait()

    def each(n, fn):
        def step(k, carry):
            fn(k)
            return carry
        lax.fori_loop(0, n, step, 0)

    def line(k):
        return g, 2 * ((y + k) % 8) + 1

    def heads_of(t):
        return pl.ds(pl.multiple_of(t * 512, 512), 512)

    slots = pl.ds(q * 4, 4)

    bar = pltpu.get_barrier_semaphore()
    rank = par * 16 + s

    def greet(k):
        to = c * ((rank + k + 1) % 32) + (1 - c) * ((2 * k + 1) % 32)
        pl.semaphore_signal(bar, inc=1, device_id=(base + to // 16, to % 16), device_id_type=MESH)

    each(16 + 15 * c, greet)

    c_conv = local(convs_hbm, convs, lsem.at[0])

    @pl.when(c == 1)
    def _():
        local(qkvw_hbm, qkvw.at[1], rsem.at[22])
        local(key_hbm.at[:, :, heads_of(par)], kall.at[slots], rsem.at[0])
        local(gatew_hbm, gatew.at[1], rsem.at[23])
        local(upw_hbm, upw.at[1], rsem.at[24])
        local(downw_hbm, downw.at[1], rsem.at[25])
        local(outw_hbm, outw.at[y, 1], rsem.at[1])
        local(val_hbm.at[:, :, heads_of(par)], vall.at[slots], rsem.at[2])
        local(tok_ref, tokall.at[s], rsem.at[3])

    slot16 = iota((16, 128), 0) % 4

    def pick(ref):
        return jnp.where(
            slot16 == 0, ref[0], jnp.where(slot16 == 1, ref[1], jnp.where(slot16 == 2, ref[2], ref[3]))
        )

    live = iota((16, 128), 1) < pick(fill_ref)
    own = pick(owner_ref).astype(F32)
    logw = logw_ref[...].astype(F32)
    for t in range(2):
        rows = [logw[j, 4 * t + h : 4 * t + h + 1, :] for h in range(4) for j in range(4)]
        wo_src[t, 0:16, :] = jnp.where(live, jnp.exp(jnp.concatenate(rows, axis=0)), 0.0)
        wo_src[t, 16:32, :] = own
    c_conv.wait()
    past = jnp.zeros((32, 192), F32)
    for k in range(3):
        past = past + convw_ref[k : k + 1, :] * convs[k].astype(F32)
    past_out[0:32, :] = past
    past_out[32:40, :] = jnp.broadcast_to(convw_ref[3:4, :], (8, 192))

    pl.semaphore_wait(bar, 16 + 15 * c)

    @pl.when(c == 0)
    def _():
        mate = (g, 2 * y + 1)

        def send_tok(k):
            remote(tok_ref, tokall.at[s], ssem.at[0], rsem.at[3], (g, 2 * ((y + k) % 8) + 1))

        each(8, send_tok)
        remote(past_out, past_in, ssem.at[3], rsem.at[5], mate)

        def send_wo(k):
            t = (par + k + 1) % 2
            remote(wo_src.at[t], wo_all.at[q], ssem.at[1], rsem.at[4], (base + t, 2 * y + 1))

        each(2, send_wo)

        def send_key(t):
            remote(key_hbm.at[:, :, heads_of(t)], kall.at[slots], ssem.at[2], rsem.at[0], (base + t, 2 * y + 1))

        def send_val(t):
            remote(val_hbm.at[:, :, heads_of(t)], vall.at[slots], ssem.at[6], rsem.at[2], (base + t, 2 * y + 1))

        send_key(1 - par)
        remote(qkvw_hbm, qkvw.at[0], ssem.at[4], rsem.at[22], mate)
        send_key(par)
        for to in (1, 7):
            remote(outw_hbm, outw.at[y, 0], ssem.at[5], rsem.at[18], line(to))
        remote(outw_hbm, outw.at[y, 0], ssem.at[7], rsem.at[1], mate)
        done(kall.at[pl.ds(0, 8)], ssem.at[2])
        send_val(1 - par)
        send_val(par)
        remote(gatew_hbm, gatew.at[0], ssem.at[8], rsem.at[23], mate)
        remote(upw_hbm, upw.at[0], ssem.at[9], rsem.at[24], mate)
        remote(downw_hbm, downw.at[0], ssem.at[10], rsem.at[25], mate)

    @pl.when(c == 1)
    def _():
        def pass_on(k):
            if k == 1:
                for to in (1, 7):
                    remote(outw_hbm, outw.at[y, 1], ssem.at[16], rsem.at[18], line(to))
                return
            done(outw.at[pl.ds(0, 2)], rsem.at[16 + k])
            if k == 2:
                done(outw.at[0], rsem.at[1])
            low, high = (y + 9 - k) % 8, (y + k - 1) % 8
            for way, at, to in ((0, low, 1), (1, high, 7)):
                rows = pl.ds(32 * way, 32) if k == 4 else pl.ds(0, 64)
                block = outw.at[at, :, rows]
                remote(block, block, ssem.at[15 + k], rsem.at[17 + k], line(to))

        def send_tok(k):
            remote(tok_ref, tokall.at[s], ssem.at[0], rsem.at[3], line(k + 1))

        each(7, send_tok)
        local(wo_src.at[par], wo_all.at[q], rsem.at[4])
        remote(wo_src.at[1 - par], wo_all.at[q], ssem.at[1], rsem.at[4], (partner, s))
        remote(key_hbm.at[:, :, heads_of(1 - par)], kall.at[slots], ssem.at[2], rsem.at[0], (partner, s))
        pass_on(1)

        done(wo_all, rsem.at[4])
        own16 = jnp.concatenate([wo_all[t, 16:20, :] for t in range(4)], axis=0)
        own_src[...] = own16.astype(BF16)
        local(own_src, own_all.at[y], rsem.at[7])

        def send_own(k):
            remote(own_src, own_all.at[y], ssem.at[5], rsem.at[7], line(k + 1))

        each(7, send_own)
        own64 = jnp.concatenate([own16] * 4, axis=0)
        lane256 = iota((64, 256), 1)
        hot = jnp.concatenate([own64, own64], axis=1) == (lane256 % 64).astype(F32)
        ohd[...] = (hot & (iota((64, 256), 0) // 16 == lane256 // 64)).astype(F32).astype(BF16)
        w64 = jnp.concatenate(
            [wo_all[t, 4 * h : 4 * h + 4, :] for h in range(4) for t in range(4)], axis=0
        )
        slot64 = iota((64, 128), 0) % 16
        for p in range(16):
            wmask[:, 128 * p : 128 * p + 128] = jnp.where(slot64 == p, w64, 0.0)

        done(past_in, rsem.at[5])
        low64 = iota((40, 128), 1) < 64
        left, right = past_in[...], past_out[...]
        taps = [
            left[:, 0:128],
            jnp.where(low64, pltpu.roll(left[:, 64:192], 64, 1), pltpu.roll(right[:, 0:128], 64, 1)),
            right[:, 64:192],
        ]

        done(qkvw, rsem.at[22])
        done(tokall, rsem.at[3])
        for i in range(16):
            xrows[2 * i : 2 * i + 2, :] = tokall[i].astype(F32)
        normed = row_norm(xrows[...], ngain_ref[...])
        fresh = mm_nt(normed, qkvw[...].reshape(384, 1024))
        for j in range(3):
            pre = taps[j][32:33] * fresh[:, 128 * j : 128 * j + 128] + taps[j][0:32]
            usrc[j] = silu(pre).astype(BF16)
        for j in range(3):
            unit = 3 * y + j
            kind = unit // 8
            head = unit % 8
            to_par = head // 4
            slot = kind * 8 + (head % 4) * 2 + par
            got = rsem.at[13 + kind]

            def send_unit(k, j=j, slot=slot, to_par=to_par, got=got):
                to = 2 * ((y + k + 1) % 8) + 1
                remote(usrc.at[j], uall.at[slot], ssem.at[3], got, (base + to_par, to))

            each(7, send_unit)

            @pl.when(to_par == par)
            def _(j=j, slot=slot, got=got):
                local(usrc.at[j], uall.at[slot], got)

            @pl.when(to_par != par)
            def _(j=j, slot=slot, got=got):
                remote(usrc.at[j], uall.at[slot], osem.at[j], got, (partner, s))

        gall[par, :, 0:16] = jax.nn.sigmoid(mm_nt(normed, mgate_ref[...]) + mbias_ref[...])
        remote(gall.at[par], gall.at[par], ssem.at[4], rsem.at[6], (partner, s))

        remote(val_hbm.at[:, :, heads_of(1 - par)], vall.at[slots], ssem.at[6], rsem.at[2], (partner, s))
        pass_on(2)

        def rows_of(kind):
            return uall[8 * kind : 8 * kind + 8].reshape(256, 128).astype(F32)

        done(uall.at[pl.ds(0, 8)], rsem.at[13])
        query = unit_rows(rows_of(0))
        done(kall, rsem.at[0])
        first = iota((32, 128), 0) < 16

        def spread(picked):
            return jnp.concatenate([jnp.where(first, picked, 0.0), jnp.where(first, 0.0, picked)], axis=1)

        def slot_rows(vec):
            hi, lo = split(vec)
            sel = mm(ohd[...], jnp.concatenate([hi, lo], axis=1))
            out = []
            for p in range(2):
                part = sel[32 * p : 32 * p + 32]
                both = [spread(part[:, 0:128]), spread(part[:, 128:256])]
                out.append(jnp.concatenate(both, axis=0).astype(BF16))
            return out

        def weigh(vec, turned=True):
            out = []
            for p, lhs in enumerate(slot_rows(vec)):
                scores = mm(lhs, kturn[p]) if turned else mm_nt(lhs, keys[p])
                hi, lo = split((scores[0:32] + scores[32:64]) * wmask[32 * p : 32 * p + 32, :])
                out.append(jnp.concatenate([hi, lo], axis=0))
            return out

        def gathered(weighed, source):
            out = []
            for p in range(2):
                prod = mm(weighed[p], source[p])
                both = prod[0:32] + prod[32:64]
                out.append(jnp.where(first, both[:, 0:128], both[:, 128:256]).astype(BF16))
            return jnp.concatenate(out, axis=0)

        def own_term(vec, source):
            return strength * source * rowsum(knew * vec)

        def summed(ref, at):
            wide = [ref[:, at + 16 * h : at + 16 * h + 16, :].reshape(128, 128) for h in range(4)]
            tot = mm(oht[...], jnp.concatenate(wide, axis=1))
            return decay * jnp.concatenate([tot[:, 128 * h : 128 * h + 128] for h in range(4)], axis=0)

        def halves(ref):
            return [ref[:, :, 256 * p : 256 * p + 256].reshape(2048, 256) for p in range(2)]

        keys = halves(kall)
        solution = jnp.zeros((256, 128), F32)
        residual = query
        direction = query
        res_norm = rowsum(residual * residual)
        for it in range(ITERS):
            last = it == ITERS - 1
            src, dst = (fsrc, fall) if last else (csrc.at[it], call.at[it])
            weighed = weigh(direction, it > 0)
            src[0:64, :] = gathered(weighed, keys)
            if last:
                src[64:128, :] = gathered(weighed, values)
            local(src, dst.at[y], rsem.at[8 + it])

            def send_c(k, it=it, src=src, dst=dst):
                remote(src, dst.at[y], ssem.at[8 + it], rsem.at[8 + it], line(k + 1))

            each(7, send_c)
            if it == 0:
                done(uall.at[pl.ds(8, 8)], rsem.at[14])
                knew = unit_rows(rows_of(1))
                done(gall.at[0], rsem.at[6])
                gboth = gall[...].reshape(64, 128)
                lane64 = iota((64, 128), 1)

                def column(at):
                    parts = [rowsum(jnp.where(lane64 == at + h, gboth, 0.0)) for h in range(4)]
                    return jnp.concatenate(parts, axis=0)

                decay = column(4 * par)
                strength = column(8 + 4 * par)
                ridge = jnp.concatenate(
                    [jnp.full((64, 1), ridge_ref[4 * par + h], F32) for h in range(4)], axis=0
                )
                done(own_all, rsem.at[7])
                owners = own_all[...].reshape(128, 128).astype(F32).T[0:64]
                oht[...] = (owners == iota((64, 128), 0).astype(F32)).astype(F32).astype(BF16)
                pass_on(3)
                for p in range(2):
                    for k in range(16):
                        kturn[p, :, 128 * k : 128 * k + 128] = kall[k, :, 256 * p : 256 * p + 256].T
            if it == 1:
                pass_on(4)
                done(uall.at[pl.ds(16, 8)], rsem.at[15])
                vnew = rows_of(2)
            if it == ITERS - 2:
                done(vall, rsem.at[2])
                values = halves(vall)
                rsrc[0:64, :] = gathered(weighed, values)
                rsrc[64:128, :] = gathered(weigh(solution), values)
                local(rsrc, rall.at[y], rsem.at[12])

                def send_r(k):
                    remote(rsrc, rall.at[y], ssem.at[12], rsem.at[12], line(k + 1))

                each(7, send_r)
            near = own_term(direction, knew) + ridge * direction
            if last:
                done(rall, rsem.at[12])
                read_x = summed(rall, 64) + step_size * summed(rall, 0)
                near_d = own_term(direction, vnew)
                near_x = own_term(solution, vnew)
            done(dst, rsem.at[8 + it])
            image = summed(dst, 0) + near
            step_size = res_norm / rowsum(direction * image)
            if not last:
                solution = solution + step_size * direction
                residual = residual - step_size * image
                next_norm = rowsum(residual * residual)
                direction = residual + (next_norm / res_norm) * direction
                res_norm = next_norm
        found = (read_x + near_x + step_size * (summed(fall, 64) + near_d)).astype(BF16)

        for p in range(2):
            for h in range(4):
                tsrc[p, h] = found[64 * h + 32 * p : 64 * h + 32 * p + 32, :]
        local(tsrc.at[par], tall.at[par], rsem.at[16])
        remote(tsrc.at[1 - par], tall.at[par], ssem.at[14], rsem.at[16], (partner, s))
        done(outw.at[0], rsem.at[21])
        done(gatew, rsem.at[23])
        done(upw, rsem.at[24])
        done(downw, rsem.at[25])
        done(tall, rsem.at[16])
        heads = jnp.concatenate([tall[h // 4, h % 4] for h in range(8)], axis=1)
        attended = mm(heads, outw[...].reshape(1024, 1024))
        mid = (xrows[...] + attended).astype(BF16)
        rows = row_norm(mid.astype(F32), mgain_ref[...])
        gate = mm_nt(rows, gatew[...].reshape(352, 1024))
        hidden = (silu(gate) * mm_nt(rows, upw[...].reshape(352, 1024))).astype(BF16)
        down = mm(hidden, downw[...].reshape(352, 1024)).astype(BF16)
        for r in range(16):
            nsrc[r] = down[2 * r : 2 * r + 2, :]
        local(nsrc.at[s], nall.at[y], rsem.at[17])

        def send_n(k):
            to = (s + k + 1) % 16
            remote(nsrc.at[to], nall.at[y], ssem.at[15], rsem.at[17], (g, to))

        each(15, send_n)
        chip = (iota((8, 32), 1) == 4 * y + iota((8, 32), 0)).astype(F32).astype(BF16)
        read4 = mm(chip, heads).astype(BF16)
        mid4 = mm(chip, mid)
        hsrc[0] = read4[0:2]
        hsrc[1] = mid4[0:2].astype(BF16)
        remote(hsrc, hall, ssem.at[20], rsem.at[26], (g, 2 * y))
        ret_ref[...] = read4[2:4]
        total = mid4[2:4]
        done(nall, rsem.at[17])
        for i in range(8):
            total = total + nall[i].astype(F32)
        lay_ref[...] = total.astype(BF16)

        done(tokall.at[pl.ds(0, 7)], ssem.at[0])
        done(wo_all.at[0], ssem.at[1])
        done(kall.at[pl.ds(0, 4)], ssem.at[2])
        done(uall.at[pl.ds(0, 21)], ssem.at[3])
        done(gall.at[0], ssem.at[4])
        done(own_all.at[pl.ds(0, 7)], ssem.at[5])
        done(vall.at[pl.ds(0, 4)], ssem.at[6])
        for it in range(ITERS - 1):
            done(call.at[it, pl.ds(0, 7)], ssem.at[8 + it])
        done(fall.at[pl.ds(0, 7)], ssem.at[11])
        done(rall.at[pl.ds(0, 7)], ssem.at[12])
        done(tall.at[0], ssem.at[14])
        done(nsrc.at[pl.ds(0, 15)], ssem.at[15])
        done(outw.at[0], ssem.at[16])
        done(outw.at[pl.ds(0, 2)], ssem.at[17])
        done(outw.at[pl.ds(0, 2)], ssem.at[18])
        done(outw.at[0], ssem.at[19])
        done(hsrc, ssem.at[20])
        for j in range(3):
            @pl.when(((3 * y + j) % 8) // 4 != par)
            def _(j=j):
                done(usrc.at[j], osem.at[j])

    @pl.when(c == 0)
    def _():
        done(hall, rsem.at[26])
        ret_ref[...] = hall[0]
        total = hall[1].astype(F32)
        done(nall, rsem.at[17])
        for i in range(8):
            total = total + nall[i].astype(F32)
        lay_ref[...] = total.astype(BF16)
        done(tokall.at[pl.ds(0, 8)], ssem.at[0])
        done(wo_all.at[pl.ds(0, 2)], ssem.at[1])
        done(past_out, ssem.at[3])
        done(qkvw.at[0], ssem.at[4])
        done(outw.at[0], ssem.at[5])
        done(vall.at[pl.ds(0, 8)], ssem.at[6])
        done(outw.at[0, 0], ssem.at[7])
        done(gatew.at[0], ssem.at[8])
        done(upw.at[0], ssem.at[9])
        done(downw.at[0], ssem.at[10])


def finish(read_ref, layer_ref, ret_ref, lay_ref):
    ret_ref[...] = read_ref[...]
    lay_ref[...] = layer_ref[...]


def body(
    tokens, norm_gain, qkv_weight, conv_weight, conv_state, mesa_gates, mesa_bias, ridge_term,
    key_cache, value_cache, log_weight, page_owner, page_fill, out_weight, mlp_gain,
    gate_weight, up_weight, down_weight,
):
    vm = pl.BlockSpec(memory_space=pltpu.VMEM)
    sm = pl.BlockSpec(memory_space=pltpu.SMEM)
    hb = pl.BlockSpec(memory_space=pltpu.HBM)
    v = pltpu.VMEM
    dma = pltpu.SemaphoreType.DMA
    pair = (jax.ShapeDtypeStruct((2, 1024), BF16), jax.ShapeDtypeStruct((2, 1024), BF16))
    read, layer = pl.pallas_call(
        kernel,
        name="layer",
        out_shape=pair,
        in_specs=[vm, vm, hb, vm, hb, vm, vm, sm, hb, hb, vm, sm, sm, hb, vm, hb, hb, hb],
        out_specs=(vm, vm),
        scratch_shapes=[
            v((2, 192, 1024), BF16), v((3, 32, 192), BF16), v((8, 2, 64, 1024), BF16),
            v((2, 176, 1024), BF16), v((2, 176, 1024), BF16), v((2, 176, 1024), BF16),
            v((16, 128, 512), BF16), v((16, 128, 512), BF16),
            v((16, 2, 1024), BF16), v((32, 1024), F32),
            v((2, 32, 128), F32), v((4, 32, 128), F32), v((64, 2048), F32),
            v((40, 192), F32), v((40, 192), F32),
            v((3, 32, 128), BF16), v((24, 32, 128), BF16), v((2, 32, 128), F32),
            v((16, 128), BF16), v((8, 16, 128), BF16), v((64, 256), BF16), v((64, 128), BF16),
            v((3, 64, 128), BF16), v((3, 8, 64, 128), BF16),
            v((128, 128), BF16), v((8, 128, 128), BF16),
            v((128, 128), BF16), v((8, 128, 128), BF16),
            v((2, 4, 32, 128), BF16), v((2, 4, 32, 128), BF16),
            v((16, 2, 1024), BF16), v((8, 2, 1024), BF16),
            v((2, 2, 1024), BF16), v((2, 2, 1024), BF16),
            v((2, 256, 2048), BF16),
            dma((1,)), dma((3,)), dma((21,)), dma((27,)),
        ],
        compiler_params=pltpu.CompilerParams(
            collective_id=0, has_side_effects=True, vmem_limit_bytes=56 * 1024 * 1024
        ),
    )(
        tokens, norm_gain.reshape(1, -1), qkv_weight.T, conv_weight, conv_state.transpose(1, 0, 2),
        mesa_gates.T, mesa_bias.reshape(1, -1), ridge_term, key_cache, value_cache, log_weight,
        page_owner, page_fill, out_weight, mlp_gain.reshape(1, -1), gate_weight.T, up_weight.T, down_weight,
    )
    return pl.pallas_call(
        finish, name="finish", out_shape=pair, in_specs=[vm, vm], out_specs=(vm, vm)
    )(read, layer)


def solution(mesh):
    return jax.shard_map(
        body,
        mesh=mesh,
        in_specs=(
            P(("group", "shard"), None),
            P(),
            P(None, "shard"),
            P(None, "shard"),
            P("group", None, "shard"),
            P(),
            P(),
            P(),
            P(("group", "shard"), None, None),
            P(("group", "shard"), None, None),
            P(("group", "shard"), None, None),
            P(("group", "shard")),
            P(("group", "shard")),
            P("shard", None),
            P(),
            P(None, "shard"),
            P(None, "shard"),
            P("shard", None),
        ),
        out_specs=(P(("group", "shard"), None), P(("group", "shard"), None)),
        check_vma=False,
    )
```

```python
import functools

import jax
import jax.numpy as jnp
from jax import lax
from jax.experimental import pallas as pl
from jax.experimental.pallas import tpu as pltpu
from jax.sharding import PartitionSpec as P

MESH = pl.DeviceIdType.MESH
F32 = jnp.float32
BF16 = jnp.bfloat16
ITERS = 4


def iota(shape, dim):
    return lax.broadcasted_iota(jnp.int32, shape, dim)


def mm(a, b):
    return jnp.dot(a, b, preferred_element_type=F32)


def mm_nt(a, b):
    return lax.dot_general(a, b, (((1,), (1,)), ((), ())), preferred_element_type=F32)


def split(v):
    hi = v.astype(BF16)
    lo = (v - hi.astype(F32)).astype(BF16)
    return hi, lo


def silu(v):
    return v / (1.0 + jnp.exp(-v))


def row_norm(wide, gain):
    factor = lax.rsqrt(jnp.mean(wide * wide, axis=-1, keepdims=True) + 1e-05)
    return (wide * factor * gain).astype(BF16)


def unit_rows(v):
    return v * lax.rsqrt(jnp.sum(v * v, axis=-1, keepdims=True) + 1e-06)


def rowsum(v):
    return jnp.sum(v, axis=-1, keepdims=True)


def kernel(
    tok_ref, ngain_ref, qkvw_hbm, convw_ref, convs_hbm, mgate_ref, mbias_ref, ridge_ref,
    key_hbm, val_hbm, logw_ref, owner_ref, fill_ref, outw_hbm, mgain_ref, gatew_hbm, upw_hbm, downw_hbm,
    ret_ref, lay_ref,
    qkvw, convs, outw, gatew, upw, downw,
    kall, vall, tokall, xrows, wo_src, wo_all, wmask, past_out, past_in,
    usrc, uall, gall, own_src, own_all, ohd, oht,
    csrc, call, rsrc, rall, fsrc, fall, tsrc, tall, nsrc, nall, hsrc, hall,
    kturn, lsem, osem, ssem, rsem,
):
    g = lax.axis_index("group")
    s = lax.axis_index("shard")
    par = g % 2
    base = g - par
    y = s // 2
    c = s % 2
    q = par * 2 + c
    partner = base + 1 - par

    def local(src, dst, sem):
        cp = pltpu.make_async_copy(src, dst, sem)
        cp.start()
        return cp

    def remote(src, dst, send, recv, dev):
        pltpu.make_async_remote_copy(
            src_ref=src, dst_ref=dst, send_sem=send, recv_sem=recv,
            device_id=dev, device_id_type=MESH,
        ).start()

    def done(ref, sem):
        pltpu.make_async_copy(ref, ref, sem).wait()

    def each(n, fn):
        def step(k, carry):
            fn(k)
            return carry
        lax.fori_loop(0, n, step, 0)

    def far(k):
        return 4 + (k % 2) * ((k + 1) // 2) - (1 - k % 2) * (k // 2)

    def line(k):
        return g, 2 * ((y + k) % 8) + 1

    def heads_of(t):
        return pl.ds(pl.multiple_of(t * 512, 512), 512)

    slots = pl.ds(q * 4, 4)

    bar = pltpu.get_barrier_semaphore()
    rank = par * 16 + s

    def greet(k):
        to = c * ((rank + k + 1) % 32) + (1 - c) * ((2 * k + 1) % 32)
        pl.semaphore_signal(bar, inc=1, device_id=(base + to // 16, to % 16), device_id_type=MESH)

    each(16 + 15 * c, greet)

    c_conv = local(convs_hbm, convs, lsem.at[0])

    @pl.when(c == 1)
    def _():
        local(qkvw_hbm, qkvw.at[1], rsem.at[22])
        local(key_hbm.at[:, :, heads_of(par)], kall.at[slots], rsem.at[0])
        local(gatew_hbm, gatew.at[1], rsem.at[23])
        local(upw_hbm, upw.at[1], rsem.at[24])
        local(downw_hbm, downw.at[1], rsem.at[25])
        local(outw_hbm, outw.at[y, 1], rsem.at[1])
        local(val_hbm.at[:, :, heads_of(par)], vall.at[slots], rsem.at[2])
        local(tok_ref, tokall.at[s], rsem.at[3])

    slot16 = iota((16, 128), 0) % 4

    def pick(ref):
        return jnp.where(
            slot16 == 0, ref[0], jnp.where(slot16 == 1, ref[1], jnp.where(slot16 == 2, ref[2], ref[3]))
        )

    live = iota((16, 128), 1) < pick(fill_ref)
    own = pick(owner_ref).astype(F32)
    logw = logw_ref[...].astype(F32)
    for t in range(2):
        rows = [logw[j, 4 * t + h : 4 * t + h + 1, :] for h in range(4) for j in range(4)]
        wo_src[t, 0:16, :] = jnp.where(live, jnp.exp(jnp.concatenate(rows, axis=0)), 0.0)
        wo_src[t, 16:32, :] = own
    c_conv.wait()
    past = jnp.zeros((32, 192), F32)
    for k in range(3):
        past = past + convw_ref[k : k + 1, :] * convs[k].astype(F32)
    past_out[0:32, :] = past
    past_out[32:40, :] = jnp.broadcast_to(convw_ref[3:4, :], (8, 192))

    pl.semaphore_wait(bar, 16 + 15 * c)

    @pl.when(c == 0)
    def _():
        mate = (g, 2 * y + 1)

        def send_tok(k):
            remote(tok_ref, tokall.at[s], ssem.at[0], rsem.at[3], line(far(k)))

        each(8, send_tok)
        remote(past_out, past_in, ssem.at[3], rsem.at[5], mate)

        def send_wo(k):
            t = (par + k + 1) % 2
            remote(wo_src.at[t], wo_all.at[q], ssem.at[1], rsem.at[4], (base + t, 2 * y + 1))

        each(2, send_wo)

        def send_key(t):
            remote(key_hbm.at[:, :, heads_of(t)], kall.at[slots], ssem.at[2], rsem.at[0], (base + t, 2 * y + 1))

        def send_val(t):
            remote(val_hbm.at[:, :, heads_of(t)], vall.at[slots], ssem.at[6], rsem.at[2], (base + t, 2 * y + 1))

        send_key(1 - par)
        remote(qkvw_hbm, qkvw.at[0], ssem.at[4], rsem.at[22], mate)
        send_key(par)
        for to in (1, 7):
            remote(outw_hbm, outw.at[y, 0], ssem.at[5], rsem.at[18], line(to))
        remote(outw_hbm, outw.at[y, 0], ssem.at[7], rsem.at[1], mate)
        done(kall.at[pl.ds(0, 8)], ssem.at[2])
        send_val(1 - par)
        send_val(par)
        remote(gatew_hbm, gatew.at[0], ssem.at[8], rsem.at[23], mate)
        remote(upw_hbm, upw.at[0], ssem.at[9], rsem.at[24], mate)
        remote(downw_hbm, downw.at[0], ssem.at[10], rsem.at[25], mate)

    @pl.when(c == 1)
    def _():
        def pass_on(k):
            if k == 1:
                for to in (1, 7):
                    remote(outw_hbm, outw.at[y, 1], ssem.at[16], rsem.at[18], line(to))
                return
            done(outw.at[pl.ds(0, 2)], rsem.at[16 + k])
            if k == 2:
                done(outw.at[0], rsem.at[1])
            low, high = (y + 9 - k) % 8, (y + k - 1) % 8
            for way, at, to in ((0, low, 1), (1, high, 7)):
                rows = pl.ds(32 * way, 32) if k == 4 else pl.ds(0, 64)
                block = outw.at[at, :, rows]
                remote(block, block, ssem.at[15 + k], rsem.at[17 + k], line(to))

        def send_tok(k):
            remote(tok_ref, tokall.at[s], ssem.at[0], rsem.at[3], line(far(k)))

        each(7, send_tok)
        local(wo_src.at[par], wo_all.at[q], rsem.at[4])
        remote(wo_src.at[1 - par], wo_all.at[q], ssem.at[1], rsem.at[4], (partner, s))
        remote(key_hbm.at[:, :, heads_of(1 - par)], kall.at[slots], ssem.at[2], rsem.at[0], (partner, s))
        pass_on(1)

        done(wo_all, rsem.at[4])
        own16 = jnp.concatenate([wo_all[t, 16:20, :] for t in range(4)], axis=0)
        own_src[...] = own16.astype(BF16)
        local(own_src, own_all.at[y], rsem.at[7])

        def send_own(k):
            remote(own_src, own_all.at[y], ssem.at[5], rsem.at[7], line(far(k)))

        each(7, send_own)
        own64 = jnp.concatenate([own16] * 4, axis=0)
        lane256 = iota((64, 256), 1)
        hot = jnp.concatenate([own64, own64], axis=1) == (lane256 % 64).astype(F32)
        ohd[...] = (hot & (iota((64, 256), 0) // 16 == lane256 // 64)).astype(F32).astype(BF16)
        w64 = jnp.concatenate(
            [wo_all[t, 4 * h : 4 * h + 4, :] for h in range(4) for t in range(4)], axis=0
        )
        slot64 = iota((64, 128), 0) % 16
        for p in range(16):
            wmask[:, 128 * p : 128 * p + 128] = jnp.where(slot64 == p, w64, 0.0)

        done(past_in, rsem.at[5])
        low64 = iota((40, 128), 1) < 64
        left, right = past_in[...], past_out[...]
        taps = [
            left[:, 0:128],
            jnp.where(low64, pltpu.roll(left[:, 64:192], 64, 1), pltpu.roll(right[:, 0:128], 64, 1)),
            right[:, 64:192],
        ]

        done(qkvw, rsem.at[22])
        done(tokall, rsem.at[3])
        for i in range(16):
            xrows[2 * i : 2 * i + 2, :] = tokall[i].astype(F32)
        normed = row_norm(xrows[...], ngain_ref[...])
        fresh = mm_nt(normed, qkvw[...].reshape(384, 1024))
        for j in range(3):
            pre = taps[j][32:33] * fresh[:, 128 * j : 128 * j + 128] + taps[j][0:32]
            usrc[j] = silu(pre).astype(BF16)
        for j in range(3):
            unit = 3 * y + j
            kind = unit // 8
            head = unit % 8
            to_par = head // 4
            slot = kind * 8 + (head % 4) * 2 + par
            got = rsem.at[13 + kind]

            def send_unit(k, j=j, slot=slot, to_par=to_par, got=got):
                to = 2 * ((y + far(k)) % 8) + 1
                remote(usrc.at[j], uall.at[slot], ssem.at[3], got, (base + to_par, to))

            each(7, send_unit)

            @pl.when(to_par == par)
            def _(j=j, slot=slot, got=got):
                local(usrc.at[j], uall.at[slot], got)

            @pl.when(to_par != par)
            def _(j=j, slot=slot, got=got):
                remote(usrc.at[j], uall.at[slot], osem.at[j], got, (partner, s))

        gall[par, :, 0:16] = jax.nn.sigmoid(mm_nt(normed, mgate_ref[...]) + mbias_ref[...])
        remote(gall.at[par], gall.at[par], ssem.at[4], rsem.at[6], (partner, s))

        remote(val_hbm.at[:, :, heads_of(1 - par)], vall.at[slots], ssem.at[6], rsem.at[2], (partner, s))
        pass_on(2)

        def rows_of(kind):
            return uall[8 * kind : 8 * kind + 8].reshape(256, 128).astype(F32)

        done(uall.at[pl.ds(0, 8)], rsem.at[13])
        query = unit_rows(rows_of(0))
        done(kall, rsem.at[0])
        first = iota((32, 128), 0) < 16

        def spread(picked):
            return jnp.concatenate([jnp.where(first, picked, 0.0), jnp.where(first, 0.0, picked)], axis=1)

        def slot_rows(vec):
            hi, lo = split(vec)
            sel = mm(ohd[...], jnp.concatenate([hi, lo], axis=1))
            out = []
            for p in range(2):
                part = sel[32 * p : 32 * p + 32]
                both = [spread(part[:, 0:128]), spread(part[:, 128:256])]
                out.append(jnp.concatenate(both, axis=0).astype(BF16))
            return out

        def weigh(vec, turned=True):
            out = []
            for p, lhs in enumerate(slot_rows(vec)):
                scores = mm(lhs, kturn[p]) if turned else mm_nt(lhs, keys[p])
                hi, lo = split((scores[0:32] + scores[32:64]) * wmask[32 * p : 32 * p + 32, :])
                out.append(jnp.concatenate([hi, lo], axis=0))
            return out

        def gathered(weighed, source):
            out = []
            for p in range(2):
                prod = mm(weighed[p], source[p])
                both = prod[0:32] + prod[32:64]
                out.append(jnp.where(first, both[:, 0:128], both[:, 128:256]).astype(BF16))
            return jnp.concatenate(out, axis=0)

        def own_term(vec, source):
            return strength * source * rowsum(knew * vec)

        def summed(ref, at):
            wide = [ref[:, at + 16 * h : at + 16 * h + 16, :].reshape(128, 128) for h in range(4)]
            tot = mm(oht[...], jnp.concatenate(wide, axis=1))
            return decay * jnp.concatenate([tot[:, 128 * h : 128 * h + 128] for h in range(4)], axis=0)

        def halves(ref):
            return [ref[:, :, 256 * p : 256 * p + 256].reshape(2048, 256) for p in range(2)]

        keys = halves(kall)
        solution = jnp.zeros((256, 128), F32)
        residual = query
        direction = query
        res_norm = rowsum(residual * residual)
        for it in range(ITERS):
            last = it == ITERS - 1
            src, dst = (fsrc, fall) if last else (csrc.at[it], call.at[it])
            weighed = weigh(direction, it > 0)
            src[0:64, :] = gathered(weighed, keys)
            if last:
                src[64:128, :] = gathered(weighed, values)
            local(src, dst.at[y], rsem.at[8 + it])

            def send_c(k, it=it, src=src, dst=dst):
                remote(src, dst.at[y], ssem.at[8 + it], rsem.at[8 + it], line(far(k)))

            each(7, send_c)
            if it == 0:
                done(uall.at[pl.ds(8, 8)], rsem.at[14])
                knew = unit_rows(rows_of(1))
                done(gall.at[0], rsem.at[6])
                gboth = gall[...].reshape(64, 128)
                lane64 = iota((64, 128), 1)

                def column(at):
                    parts = [rowsum(jnp.where(lane64 == at + h, gboth, 0.0)) for h in range(4)]
                    return jnp.concatenate(parts, axis=0)

                decay = column(4 * par)
                strength = column(8 + 4 * par)
                ridge = jnp.concatenate(
                    [jnp.full((64, 1), ridge_ref[4 * par + h], F32) for h in range(4)], axis=0
                )
                done(own_all, rsem.at[7])
                owners = own_all[...].reshape(128, 128).astype(F32).T[0:64]
                oht[...] = (owners == iota((64, 128), 0).astype(F32)).astype(F32).astype(BF16)
                pass_on(3)
                for p in range(2):
                    for k in range(16):
                        kturn[p, :, 128 * k : 128 * k + 128] = kall[k, :, 256 * p : 256 * p + 256].T
            if it == 1:
                pass_on(4)
                done(uall.at[pl.ds(16, 8)], rsem.at[15])
                vnew = rows_of(2)
            if it == ITERS - 2:
                done(vall, rsem.at[2])
                values = halves(vall)
                rsrc[0:64, :] = gathered(weighed, values)
                rsrc[64:128, :] = gathered(weigh(solution), values)
                local(rsrc, rall.at[y], rsem.at[12])

                def send_r(k):
                    remote(rsrc, rall.at[y], ssem.at[12], rsem.at[12], line(far(k)))

                each(7, send_r)
            near = own_term(direction, knew) + ridge * direction
            if last:
                done(rall, rsem.at[12])
                read_x = summed(rall, 64) + step_size * summed(rall, 0)
                near_d = own_term(direction, vnew)
                near_x = own_term(solution, vnew)
            done(dst, rsem.at[8 + it])
            image = summed(dst, 0) + near
            step_size = res_norm / rowsum(direction * image)
            if not last:
                solution = solution + step_size * direction
                residual = residual - step_size * image
                next_norm = rowsum(residual * residual)
                direction = residual + (next_norm / res_norm) * direction
                res_norm = next_norm
        found = (read_x + near_x + step_size * (summed(fall, 64) + near_d)).astype(BF16)

        for p in range(2):
            for h in range(4):
                tsrc[p, h] = found[64 * h + 32 * p : 64 * h + 32 * p + 32, :]
        local(tsrc.at[par], tall.at[par], rsem.at[16])
        remote(tsrc.at[1 - par], tall.at[par], ssem.at[14], rsem.at[16], (partner, s))
        done(outw.at[0], rsem.at[21])
        done(gatew, rsem.at[23])
        done(upw, rsem.at[24])
        done(downw, rsem.at[25])
        done(tall, rsem.at[16])
        heads = jnp.concatenate([tall[h // 4, h % 4] for h in range(8)], axis=1)
        attended = mm(heads, outw[...].reshape(1024, 1024))
        mid = (xrows[...] + attended).astype(BF16)
        rows = row_norm(mid.astype(F32), mgain_ref[...])
        gate = mm_nt(rows, gatew[...].reshape(352, 1024))
        hidden = (silu(gate) * mm_nt(rows, upw[...].reshape(352, 1024))).astype(BF16)
        down = mm(hidden, downw[...].reshape(352, 1024)).astype(BF16)
        for r in range(16):
            nsrc[r] = down[2 * r : 2 * r + 2, :]
        local(nsrc.at[s], nall.at[y], rsem.at[17])

        def send_n(k):
            to = 2 * ((y + far(k // 2)) % 8) + k % 2
            remote(nsrc.at[to], nall.at[y], ssem.at[15], rsem.at[17], (g, to))

        each(15, send_n)
        chip = (iota((8, 32), 1) == 4 * y + iota((8, 32), 0)).astype(F32).astype(BF16)
        read4 = mm(chip, heads).astype(BF16)
        mid4 = mm(chip, mid)
        hsrc[0] = read4[0:2]
        hsrc[1] = mid4[0:2].astype(BF16)
        remote(hsrc, hall, ssem.at[20], rsem.at[26], (g, 2 * y))
        ret_ref[...] = read4[2:4]
        total = mid4[2:4]
        done(nall, rsem.at[17])
        for i in range(8):
            total = total + nall[i].astype(F32)
        lay_ref[...] = total.astype(BF16)

        done(tokall.at[pl.ds(0, 7)], ssem.at[0])
        done(wo_all.at[0], ssem.at[1])
        done(kall.at[pl.ds(0, 4)], ssem.at[2])
        done(uall.at[pl.ds(0, 21)], ssem.at[3])
        done(gall.at[0], ssem.at[4])
        done(own_all.at[pl.ds(0, 7)], ssem.at[5])
        done(vall.at[pl.ds(0, 4)], ssem.at[6])
        for it in range(ITERS - 1):
            done(call.at[it, pl.ds(0, 7)], ssem.at[8 + it])
        done(fall.at[pl.ds(0, 7)], ssem.at[11])
        done(rall.at[pl.ds(0, 7)], ssem.at[12])
        done(tall.at[0], ssem.at[14])
        done(nsrc.at[pl.ds(0, 15)], ssem.at[15])
        done(outw.at[0], ssem.at[16])
        done(outw.at[pl.ds(0, 2)], ssem.at[17])
        done(outw.at[pl.ds(0, 2)], ssem.at[18])
        done(outw.at[0], ssem.at[19])
        done(hsrc, ssem.at[20])
        for j in range(3):
            @pl.when(((3 * y + j) % 8) // 4 != par)
            def _(j=j):
                done(usrc.at[j], osem.at[j])

    @pl.when(c == 0)
    def _():
        done(hall, rsem.at[26])
        ret_ref[...] = hall[0]
        total = hall[1].astype(F32)
        done(nall, rsem.at[17])
        for i in range(8):
            total = total + nall[i].astype(F32)
        lay_ref[...] = total.astype(BF16)
        done(tokall.at[pl.ds(0, 8)], ssem.at[0])
        done(wo_all.at[pl.ds(0, 2)], ssem.at[1])
        done(past_out, ssem.at[3])
        done(qkvw.at[0], ssem.at[4])
        done(outw.at[0], ssem.at[5])
        done(vall.at[pl.ds(0, 8)], ssem.at[6])
        done(outw.at[0, 0], ssem.at[7])
        done(gatew.at[0], ssem.at[8])
        done(upw.at[0], ssem.at[9])
        done(downw.at[0], ssem.at[10])


def finish(read_ref, layer_ref, ret_ref, lay_ref):
    ret_ref[...] = read_ref[...]
    lay_ref[...] = layer_ref[...]


def body(
    tokens, norm_gain, qkv_weight, conv_weight, conv_state, mesa_gates, mesa_bias, ridge_term,
    key_cache, value_cache, log_weight, page_owner, page_fill, out_weight, mlp_gain,
    gate_weight, up_weight, down_weight,
):
    vm = pl.BlockSpec(memory_space=pltpu.VMEM)
    sm = pl.BlockSpec(memory_space=pltpu.SMEM)
    hb = pl.BlockSpec(memory_space=pltpu.HBM)
    v = pltpu.VMEM
    dma = pltpu.SemaphoreType.DMA
    pair = (jax.ShapeDtypeStruct((2, 1024), BF16), jax.ShapeDtypeStruct((2, 1024), BF16))
    read, layer = pl.pallas_call(
        kernel,
        name="layer",
        out_shape=pair,
        in_specs=[vm, vm, hb, vm, hb, vm, vm, sm, hb, hb, vm, sm, sm, hb, vm, hb, hb, hb],
        out_specs=(vm, vm),
        scratch_shapes=[
            v((2, 192, 1024), BF16), v((3, 32, 192), BF16), v((8, 2, 64, 1024), BF16),
            v((2, 176, 1024), BF16), v((2, 176, 1024), BF16), v((2, 176, 1024), BF16),
            v((16, 128, 512), BF16), v((16, 128, 512), BF16),
            v((16, 2, 1024), BF16), v((32, 1024), F32),
            v((2, 32, 128), F32), v((4, 32, 128), F32), v((64, 2048), F32),
            v((40, 192), F32), v((40, 192), F32),
            v((3, 32, 128), BF16), v((24, 32, 128), BF16), v((2, 32, 128), F32),
            v((16, 128), BF16), v((8, 16, 128), BF16), v((64, 256), BF16), v((64, 128), BF16),
            v((3, 64, 128), BF16), v((3, 8, 64, 128), BF16),
            v((128, 128), BF16), v((8, 128, 128), BF16),
            v((128, 128), BF16), v((8, 128, 128), BF16),
            v((2, 4, 32, 128), BF16), v((2, 4, 32, 128), BF16),
            v((16, 2, 1024), BF16), v((8, 2, 1024), BF16),
            v((2, 2, 1024), BF16), v((2, 2, 1024), BF16),
            v((2, 256, 2048), BF16),
            dma((1,)), dma((3,)), dma((21,)), dma((27,)),
        ],
        compiler_params=pltpu.CompilerParams(
            collective_id=0, has_side_effects=True, vmem_limit_bytes=56 * 1024 * 1024
        ),
    )(
        tokens, norm_gain.reshape(1, -1), qkv_weight.T, conv_weight, conv_state.transpose(1, 0, 2),
        mesa_gates.T, mesa_bias.reshape(1, -1), ridge_term, key_cache, value_cache, log_weight,
        page_owner, page_fill, out_weight, mlp_gain.reshape(1, -1), gate_weight.T, up_weight.T, down_weight,
    )
    return pl.pallas_call(
        finish, name="finish", out_shape=pair, in_specs=[vm, vm], out_specs=(vm, vm)
    )(read, layer)


def solution(mesh):
    return jax.shard_map(
        body,
        mesh=mesh,
        in_specs=(
            P(("group", "shard"), None),
            P(),
            P(None, "shard"),
            P(None, "shard"),
            P("group", None, "shard"),
            P(),
            P(),
            P(),
            P(("group", "shard"), None, None),
            P(("group", "shard"), None, None),
            P(("group", "shard"), None, None),
            P(("group", "shard")),
            P(("group", "shard")),
            P("shard", None),
            P(),
            P(None, "shard"),
            P(None, "shard"),
            P("shard", None),
        ),
        out_specs=(P(("group", "shard"), None), P(("group", "shard"), None)),
        check_vma=False,
    )
```

```python
import functools

import jax
import jax.numpy as jnp
from jax import lax
from jax.experimental import pallas as pl
from jax.experimental.pallas import tpu as pltpu
from jax.sharding import PartitionSpec as P

MESH = pl.DeviceIdType.MESH
F32 = jnp.float32
BF16 = jnp.bfloat16
ITERS = 4


def iota(shape, dim):
    return lax.broadcasted_iota(jnp.int32, shape, dim)


def mm(a, b):
    return jnp.dot(a, b, preferred_element_type=F32)


def mm_nt(a, b):
    return lax.dot_general(a, b, (((1,), (1,)), ((), ())), preferred_element_type=F32)


def split(v):
    hi = v.astype(BF16)
    lo = (v - hi.astype(F32)).astype(BF16)
    return hi, lo


def silu(v):
    return v / (1.0 + jnp.exp(-v))


def row_norm(wide, gain):
    factor = lax.rsqrt(jnp.mean(wide * wide, axis=-1, keepdims=True) + 1e-05)
    return (wide * factor * gain).astype(BF16)


def unit_rows(v):
    return v * lax.rsqrt(jnp.sum(v * v, axis=-1, keepdims=True) + 1e-06)


def rowsum(v):
    return jnp.sum(v, axis=-1, keepdims=True)


def kernel(
    tok_ref, ngain_ref, qkvw_hbm, convw_ref, convs_hbm, mgate_ref, mbias_ref, ridge_ref,
    key_hbm, val_hbm, logw_ref, owner_ref, fill_ref, outw_hbm, mgain_ref, gatew_hbm, upw_hbm, downw_hbm,
    ret_ref, lay_ref,
    qkvw, convs, outw, gatew, upw, downw,
    kall, vall, tokall, xrows, wo_src, wo_all, wmask, past_out, past_in,
    usrc, uall, gall, own_src, own_all, ohd, oht,
    csrc, call, rsrc, rall, fsrc, fall, tsrc, tall, nsrc, nall, hsrc, hall,
    kturn, lsem, osem, ssem, rsem,
):
    g = lax.axis_index("group")
    s = lax.axis_index("shard")
    par = g % 2
    base = g - par
    y = s // 2
    c = s % 2
    q = par * 2 + c
    partner = base + 1 - par

    def local(src, dst, sem):
        cp = pltpu.make_async_copy(src, dst, sem)
        cp.start()
        return cp

    def remote(src, dst, send, recv, dev):
        pltpu.make_async_remote_copy(
            src_ref=src, dst_ref=dst, send_sem=send, recv_sem=recv,
            device_id=dev, device_id_type=MESH,
        ).start()

    def done(ref, sem):
        pltpu.make_async_copy(ref, ref, sem).wait()

    def each(n, fn):
        def step(k, carry):
            fn(k)
            return carry
        lax.fori_loop(0, n, step, 0)

    def far(k):
        return 4 + (k % 2) * ((k + 1) // 2) - (1 - k % 2) * (k // 2)

    def line(k):
        return g, 2 * ((y + k) % 8) + 1

    def heads_of(t):
        return pl.ds(pl.multiple_of(t * 512, 512), 512)

    slots = pl.ds(q * 4, 4)

    bar = pltpu.get_barrier_semaphore()
    rank = par * 16 + s

    def greet(k):
        to = c * ((rank + k + 1) % 32) + (1 - c) * ((2 * k + 1) % 32)
        pl.semaphore_signal(bar, inc=1, device_id=(base + to // 16, to % 16), device_id_type=MESH)

    each(16 + 15 * c, greet)

    c_conv = local(convs_hbm, convs, lsem.at[0])

    @pl.when(c == 1)
    def _():
        local(qkvw_hbm, qkvw.at[1], rsem.at[22])
        local(key_hbm.at[:, :, heads_of(par)], kall.at[slots], rsem.at[0])
        local(gatew_hbm, gatew.at[1], rsem.at[23])
        local(upw_hbm, upw.at[1], rsem.at[24])
        local(downw_hbm, downw.at[1], rsem.at[25])
        local(outw_hbm, outw.at[y, 1], rsem.at[1])
        local(val_hbm.at[:, :, heads_of(par)], vall.at[slots], rsem.at[2])
        local(tok_ref, tokall.at[s], rsem.at[3])

    slot16 = iota((16, 128), 0) % 4

    def pick(ref):
        return jnp.where(
            slot16 == 0, ref[0], jnp.where(slot16 == 1, ref[1], jnp.where(slot16 == 2, ref[2], ref[3]))
        )

    live = iota((16, 128), 1) < pick(fill_ref)
    own = pick(owner_ref).astype(F32)
    logw = logw_ref[...].astype(F32)
    for t in range(2):
        rows = [logw[j, 4 * t + h : 4 * t + h + 1, :] for h in range(4) for j in range(4)]
        wo_src[t, 0:16, :] = jnp.where(live, jnp.exp(jnp.concatenate(rows, axis=0)), 0.0)
        wo_src[t, 16:32, :] = own
    c_conv.wait()
    past = jnp.zeros((32, 192), F32)
    for k in range(3):
        past = past + convw_ref[k : k + 1, :] * convs[k].astype(F32)
    past_out[0:32, :] = past
    past_out[32:40, :] = jnp.broadcast_to(convw_ref[3:4, :], (8, 192))

    pl.semaphore_wait(bar, 16 + 15 * c)

    @pl.when(c == 0)
    def _():
        mate = (g, 2 * y + 1)

        def send_tok(k):
            remote(tok_ref, tokall.at[s], ssem.at[0], rsem.at[3], line(far(k)))

        each(8, send_tok)
        remote(past_out, past_in, ssem.at[3], rsem.at[5], mate)

        def send_wo(k):
            t = (par + k + 1) % 2
            remote(wo_src.at[t], wo_all.at[q], ssem.at[1], rsem.at[4], (base + t, 2 * y + 1))

        each(2, send_wo)

        def send_key(t):
            remote(key_hbm.at[:, :, heads_of(t)], kall.at[slots], ssem.at[2], rsem.at[0], (base + t, 2 * y + 1))

        def send_val(t):
            remote(val_hbm.at[:, :, heads_of(t)], vall.at[slots], ssem.at[6], rsem.at[2], (base + t, 2 * y + 1))

        send_key(1 - par)
        remote(qkvw_hbm, qkvw.at[0], ssem.at[4], rsem.at[22], mate)
        send_key(par)
        for to in (1, 7):
            remote(outw_hbm, outw.at[y, 0], ssem.at[5], rsem.at[18], line(to))
        remote(outw_hbm, outw.at[y, 0], ssem.at[7], rsem.at[1], mate)
        done(kall.at[pl.ds(0, 8)], ssem.at[2])
        send_val(1 - par)
        send_val(par)
        remote(gatew_hbm, gatew.at[0], ssem.at[8], rsem.at[23], mate)
        remote(upw_hbm, upw.at[0], ssem.at[9], rsem.at[24], mate)
        remote(downw_hbm, downw.at[0], ssem.at[10], rsem.at[25], mate)

    @pl.when(c == 1)
    def _():
        def pass_on(k):
            if k == 1:
                for to in (1, 7):
                    remote(outw_hbm, outw.at[y, 1], ssem.at[16], rsem.at[18], line(to))
                return
            done(outw.at[pl.ds(0, 2)], rsem.at[16 + k])
            if k == 2:
                done(outw.at[0], rsem.at[1])
            low, high = (y + 9 - k) % 8, (y + k - 1) % 8
            for way, at, to in ((0, low, 1), (1, high, 7)):
                rows = pl.ds(32 * way, 32) if k == 4 else pl.ds(0, 64)
                block = outw.at[at, :, rows]
                remote(block, block, ssem.at[15 + k], rsem.at[17 + k], line(to))

        def send_tok(k):
            remote(tok_ref, tokall.at[s], ssem.at[0], rsem.at[3], line(far(k)))

        each(7, send_tok)
        local(wo_src.at[par], wo_all.at[q], rsem.at[4])
        remote(wo_src.at[1 - par], wo_all.at[q], ssem.at[1], rsem.at[4], (partner, s))
        remote(key_hbm.at[:, :, heads_of(1 - par)], kall.at[slots], ssem.at[2], rsem.at[0], (partner, s))
        pass_on(1)

        done(wo_all, rsem.at[4])
        own16 = jnp.concatenate([wo_all[t, 16:20, :] for t in range(4)], axis=0)
        own_src[...] = own16.astype(BF16)
        local(own_src, own_all.at[y], rsem.at[7])

        def send_own(k):
            remote(own_src, own_all.at[y], ssem.at[5], rsem.at[7], line(far(k)))

        each(7, send_own)
        own64 = jnp.concatenate([own16] * 4, axis=0)
        lane256 = iota((64, 256), 1)
        hot = jnp.concatenate([own64, own64], axis=1) == (lane256 % 64).astype(F32)
        ohd[...] = (hot & (iota((64, 256), 0) // 16 == lane256 // 64)).astype(F32).astype(BF16)
        w64 = jnp.concatenate(
            [wo_all[t, 4 * h : 4 * h + 4, :] for h in range(4) for t in range(4)], axis=0
        )
        slot64 = iota((64, 128), 0) % 16
        for p in range(16):
            wmask[:, 128 * p : 128 * p + 128] = jnp.where(slot64 == p, w64, 0.0)

        done(past_in, rsem.at[5])
        low64 = iota((40, 128), 1) < 64
        left, right = past_in[...], past_out[...]
        taps = [
            left[:, 0:128],
            jnp.where(low64, pltpu.roll(left[:, 64:192], 64, 1), pltpu.roll(right[:, 0:128], 64, 1)),
            right[:, 64:192],
        ]

        done(qkvw, rsem.at[22])
        done(tokall, rsem.at[3])
        for i in range(16):
            xrows[2 * i : 2 * i + 2, :] = tokall[i].astype(F32)
        normed = row_norm(xrows[...], ngain_ref[...])
        fresh = mm_nt(normed, qkvw[...].reshape(384, 1024))
        for j in range(3):
            pre = taps[j][32:33] * fresh[:, 128 * j : 128 * j + 128] + taps[j][0:32]
            usrc[j] = silu(pre).astype(BF16)
        def send_units(k):
            to = 2 * ((y + far(k)) % 8) + 1
            for j in range(3):
                unit = 3 * y + j
                head = unit % 8
                slot = (unit // 8) * 8 + (head % 4) * 2 + par
                remote(usrc.at[j], uall.at[slot], ssem.at[3], rsem.at[13 + unit // 8], (base + head // 4, to))

        each(7, send_units)
        for j in range(3):
            unit = 3 * y + j
            kind = unit // 8
            head = unit % 8
            to_par = head // 4
            slot = kind * 8 + (head % 4) * 2 + par
            got = rsem.at[13 + kind]

            @pl.when(to_par == par)
            def _(j=j, slot=slot, got=got):
                local(usrc.at[j], uall.at[slot], got)

            @pl.when(to_par != par)
            def _(j=j, slot=slot, got=got):
                remote(usrc.at[j], uall.at[slot], osem.at[j], got, (partner, s))

        gall[par, :, 0:16] = jax.nn.sigmoid(mm_nt(normed, mgate_ref[...]) + mbias_ref[...])
        remote(gall.at[par], gall.at[par], ssem.at[4], rsem.at[6], (partner, s))

        remote(val_hbm.at[:, :, heads_of(1 - par)], vall.at[slots], ssem.at[6], rsem.at[2], (partner, s))
        pass_on(2)

        def rows_of(kind):
            return uall[8 * kind : 8 * kind + 8].reshape(256, 128).astype(F32)

        done(uall.at[pl.ds(0, 8)], rsem.at[13])
        query = unit_rows(rows_of(0))
        done(kall, rsem.at[0])
        first = iota((32, 128), 0) < 16

        def spread(picked):
            return jnp.concatenate([jnp.where(first, picked, 0.0), jnp.where(first, 0.0, picked)], axis=1)

        def slot_rows(vec):
            hi, lo = split(vec)
            sel = mm(ohd[...], jnp.concatenate([hi, lo], axis=1))
            out = []
            for p in range(2):
                part = sel[32 * p : 32 * p + 32]
                both = [spread(part[:, 0:128]), spread(part[:, 128:256])]
                out.append(jnp.concatenate(both, axis=0).astype(BF16))
            return out

        def weigh(vec, turned=True):
            out = []
            for p, lhs in enumerate(slot_rows(vec)):
                scores = mm(lhs, kturn[p]) if turned else mm_nt(lhs, keys[p])
                hi, lo = split((scores[0:32] + scores[32:64]) * wmask[32 * p : 32 * p + 32, :])
                out.append(jnp.concatenate([hi, lo], axis=0))
            return out

        def gathered(weighed, source):
            out = []
            for p in range(2):
                prod = mm(weighed[p], source[p])
                both = prod[0:32] + prod[32:64]
                out.append(jnp.where(first, both[:, 0:128], both[:, 128:256]).astype(BF16))
            return jnp.concatenate(out, axis=0)

        def own_term(vec, source):
            return strength * source * rowsum(knew * vec)

        def summed(ref, at):
            wide = [ref[:, at + 16 * h : at + 16 * h + 16, :].reshape(128, 128) for h in range(4)]
            tot = mm(oht[...], jnp.concatenate(wide, axis=1))
            return decay * jnp.concatenate([tot[:, 128 * h : 128 * h + 128] for h in range(4)], axis=0)

        def halves(ref):
            return [ref[:, :, 256 * p : 256 * p + 256].reshape(2048, 256) for p in range(2)]

        keys = halves(kall)
        solution = jnp.zeros((256, 128), F32)
        residual = query
        direction = query
        res_norm = rowsum(residual * residual)
        for it in range(ITERS):
            last = it == ITERS - 1
            src, dst = (fsrc, fall) if last else (csrc.at[it], call.at[it])
            weighed = weigh(direction, it > 0)
            src[0:64, :] = gathered(weighed, keys)
            if last:
                src[64:128, :] = gathered(weighed, values)
            local(src, dst.at[y], rsem.at[8 + it])

            def send_c(k, it=it, src=src, dst=dst):
                remote(src, dst.at[y], ssem.at[8 + it], rsem.at[8 + it], line(far(k)))

            each(7, send_c)
            if it == 0:
                done(uall.at[pl.ds(8, 8)], rsem.at[14])
                knew = unit_rows(rows_of(1))
                done(gall.at[0], rsem.at[6])
                gboth = gall[...].reshape(64, 128)
                lane64 = iota((64, 128), 1)

                def column(at):
                    parts = [rowsum(jnp.where(lane64 == at + h, gboth, 0.0)) for h in range(4)]
                    return jnp.concatenate(parts, axis=0)

                decay = column(4 * par)
                strength = column(8 + 4 * par)
                ridge = jnp.concatenate(
                    [jnp.full((64, 1), ridge_ref[4 * par + h], F32) for h in range(4)], axis=0
                )
                done(own_all, rsem.at[7])
                owners = own_all[...].reshape(128, 128).astype(F32).T[0:64]
                oht[...] = (owners == iota((64, 128), 0).astype(F32)).astype(F32).astype(BF16)
                pass_on(3)
                for p in range(2):
                    for k in range(16):
                        kturn[p, :, 128 * k : 128 * k + 128] = kall[k, :, 256 * p : 256 * p + 256].T
            if it == 1:
                pass_on(4)
                done(uall.at[pl.ds(16, 8)], rsem.at[15])
                vnew = rows_of(2)
            if it == ITERS - 2:
                done(vall, rsem.at[2])
                values = halves(vall)
                rsrc[0:64, :] = gathered(weighed, values)
                rsrc[64:128, :] = gathered(weigh(solution), values)
                local(rsrc, rall.at[y], rsem.at[12])

                def send_r(k):
                    remote(rsrc, rall.at[y], ssem.at[12], rsem.at[12], line(far(k)))

                each(7, send_r)
            near = own_term(direction, knew) + ridge * direction
            if last:
                done(rall, rsem.at[12])
                read_x = summed(rall, 64) + step_size * summed(rall, 0)
                near_d = own_term(direction, vnew)
                near_x = own_term(solution, vnew)
            done(dst, rsem.at[8 + it])
            image = summed(dst, 0) + near
            step_size = res_norm / rowsum(direction * image)
            if not last:
                solution = solution + step_size * direction
                residual = residual - step_size * image
                next_norm = rowsum(residual * residual)
                direction = residual + (next_norm / res_norm) * direction
                res_norm = next_norm
        found = (read_x + near_x + step_size * (summed(fall, 64) + near_d)).astype(BF16)

        for p in range(2):
            for h in range(4):
                tsrc[p, h] = found[64 * h + 32 * p : 64 * h + 32 * p + 32, :]
        local(tsrc.at[par], tall.at[par], rsem.at[16])
        remote(tsrc.at[1 - par], tall.at[par], ssem.at[14], rsem.at[16], (partner, s))
        done(outw.at[0], rsem.at[21])
        done(gatew, rsem.at[23])
        done(upw, rsem.at[24])
        done(downw, rsem.at[25])
        done(tall, rsem.at[16])
        heads = jnp.concatenate([tall[h // 4, h % 4] for h in range(8)], axis=1)
        attended = mm(heads, outw[...].reshape(1024, 1024))
        mid = (xrows[...] + attended).astype(BF16)
        rows = row_norm(mid.astype(F32), mgain_ref[...])
        gate = mm_nt(rows, gatew[...].reshape(352, 1024))
        hidden = (silu(gate) * mm_nt(rows, upw[...].reshape(352, 1024))).astype(BF16)
        down = mm(hidden, downw[...].reshape(352, 1024)).astype(BF16)
        for r in range(16):
            nsrc[r] = down[2 * r : 2 * r + 2, :]
        local(nsrc.at[s], nall.at[y], rsem.at[17])

        def send_n(k):
            to = 2 * ((y + far(k // 2)) % 8) + k % 2
            remote(nsrc.at[to], nall.at[y], ssem.at[15], rsem.at[17], (g, to))

        each(15, send_n)
        chip = (iota((8, 32), 1) == 4 * y + iota((8, 32), 0)).astype(F32).astype(BF16)
        read4 = mm(chip, heads).astype(BF16)
        mid4 = mm(chip, mid)
        hsrc[0] = read4[0:2]
        hsrc[1] = mid4[0:2].astype(BF16)
        remote(hsrc, hall, ssem.at[20], rsem.at[26], (g, 2 * y))
        ret_ref[...] = read4[2:4]
        total = mid4[2:4]
        done(nall, rsem.at[17])
        for i in range(8):
            total = total + nall[i].astype(F32)
        lay_ref[...] = total.astype(BF16)

        done(tokall.at[pl.ds(0, 7)], ssem.at[0])
        done(wo_all.at[0], ssem.at[1])
        done(kall.at[pl.ds(0, 4)], ssem.at[2])
        done(uall.at[pl.ds(0, 21)], ssem.at[3])
        done(gall.at[0], ssem.at[4])
        done(own_all.at[pl.ds(0, 7)], ssem.at[5])
        done(vall.at[pl.ds(0, 4)], ssem.at[6])
        for it in range(ITERS - 1):
            done(call.at[it, pl.ds(0, 7)], ssem.at[8 + it])
        done(fall.at[pl.ds(0, 7)], ssem.at[11])
        done(rall.at[pl.ds(0, 7)], ssem.at[12])
        done(tall.at[0], ssem.at[14])
        done(nsrc.at[pl.ds(0, 15)], ssem.at[15])
        done(outw.at[0], ssem.at[16])
        done(outw.at[pl.ds(0, 2)], ssem.at[17])
        done(outw.at[pl.ds(0, 2)], ssem.at[18])
        done(outw.at[0], ssem.at[19])
        done(hsrc, ssem.at[20])
        for j in range(3):
            @pl.when(((3 * y + j) % 8) // 4 != par)
            def _(j=j):
                done(usrc.at[j], osem.at[j])

    @pl.when(c == 0)
    def _():
        done(hall, rsem.at[26])
        ret_ref[...] = hall[0]
        total = hall[1].astype(F32)
        done(nall, rsem.at[17])
        for i in range(8):
            total = total + nall[i].astype(F32)
        lay_ref[...] = total.astype(BF16)
        done(tokall.at[pl.ds(0, 8)], ssem.at[0])
        done(wo_all.at[pl.ds(0, 2)], ssem.at[1])
        done(past_out, ssem.at[3])
        done(qkvw.at[0], ssem.at[4])
        done(outw.at[0], ssem.at[5])
        done(vall.at[pl.ds(0, 8)], ssem.at[6])
        done(outw.at[0, 0], ssem.at[7])
        done(gatew.at[0], ssem.at[8])
        done(upw.at[0], ssem.at[9])
        done(downw.at[0], ssem.at[10])


def finish(read_ref, layer_ref, ret_ref, lay_ref):
    ret_ref[...] = read_ref[...]
    lay_ref[...] = layer_ref[...]


def body(
    tokens, norm_gain, qkv_weight, conv_weight, conv_state, mesa_gates, mesa_bias, ridge_term,
    key_cache, value_cache, log_weight, page_owner, page_fill, out_weight, mlp_gain,
    gate_weight, up_weight, down_weight,
):
    vm = pl.BlockSpec(memory_space=pltpu.VMEM)
    sm = pl.BlockSpec(memory_space=pltpu.SMEM)
    hb = pl.BlockSpec(memory_space=pltpu.HBM)
    v = pltpu.VMEM
    dma = pltpu.SemaphoreType.DMA
    pair = (jax.ShapeDtypeStruct((2, 1024), BF16), jax.ShapeDtypeStruct((2, 1024), BF16))
    read, layer = pl.pallas_call(
        kernel,
        name="layer",
        out_shape=pair,
        in_specs=[vm, vm, hb, vm, hb, vm, vm, sm, hb, hb, vm, sm, sm, hb, vm, hb, hb, hb],
        out_specs=(vm, vm),
        scratch_shapes=[
            v((2, 192, 1024), BF16), v((3, 32, 192), BF16), v((8, 2, 64, 1024), BF16),
            v((2, 176, 1024), BF16), v((2, 176, 1024), BF16), v((2, 176, 1024), BF16),
            v((16, 128, 512), BF16), v((16, 128, 512), BF16),
            v((16, 2, 1024), BF16), v((32, 1024), F32),
            v((2, 32, 128), F32), v((4, 32, 128), F32), v((64, 2048), F32),
            v((40, 192), F32), v((40, 192), F32),
            v((3, 32, 128), BF16), v((24, 32, 128), BF16), v((2, 32, 128), F32),
            v((16, 128), BF16), v((8, 16, 128), BF16), v((64, 256), BF16), v((64, 128), BF16),
            v((3, 64, 128), BF16), v((3, 8, 64, 128), BF16),
            v((128, 128), BF16), v((8, 128, 128), BF16),
            v((128, 128), BF16), v((8, 128, 128), BF16),
            v((2, 4, 32, 128), BF16), v((2, 4, 32, 128), BF16),
            v((16, 2, 1024), BF16), v((8, 2, 1024), BF16),
            v((2, 2, 1024), BF16), v((2, 2, 1024), BF16),
            v((2, 256, 2048), BF16),
            dma((1,)), dma((3,)), dma((21,)), dma((27,)),
        ],
        compiler_params=pltpu.CompilerParams(
            collective_id=0, has_side_effects=True, vmem_limit_bytes=56 * 1024 * 1024
        ),
    )(
        tokens, norm_gain.reshape(1, -1), qkv_weight.T, conv_weight, conv_state.transpose(1, 0, 2),
        mesa_gates.T, mesa_bias.reshape(1, -1), ridge_term, key_cache, value_cache, log_weight,
        page_owner, page_fill, out_weight, mlp_gain.reshape(1, -1), gate_weight.T, up_weight.T, down_weight,
    )
    return pl.pallas_call(
        finish, name="finish", out_shape=pair, in_specs=[vm, vm], out_specs=(vm, vm)
    )(read, layer)


def solution(mesh):
    return jax.shard_map(
        body,
        mesh=mesh,
        in_specs=(
            P(("group", "shard"), None),
            P(),
            P(None, "shard"),
            P(None, "shard"),
            P("group", None, "shard"),
            P(),
            P(),
            P(),
            P(("group", "shard"), None, None),
            P(("group", "shard"), None, None),
            P(("group", "shard"), None, None),
            P(("group", "shard")),
            P(("group", "shard")),
            P("shard", None),
            P(),
            P(None, "shard"),
            P(None, "shard"),
            P("shard", None),
        ),
        out_specs=(P(("group", "shard"), None), P(("group", "shard"), None)),
        check_vma=False,
    )
```
